32 devices in a mesh: tm: 4 (over y, x), space: 8 (over z, core).
Axes of the slice: x: 2, y: 2, z: 4, core: 2. Of those that a mesh axis runs over, the one named last changes fastest.
Arguments:
- signal: bfloat16 [16, 256, 512], P('space', None, 'tm'), may hold values from -6 to 6
- source_boxes: int32 [16, 12], replicated, may hold values from 0 to 15
- near_boxes: int32 [16, 8], replicated, may hold values from 0 to 15, as said below
- trans_kernel: float32 [12, 256, 128], P(None, 'space'), may hold values from -0.15625 to 0.15625
- near_kernel: float32 [8, 128], replicated, may hold values from -0.1875 to 0.1875
Outputs:
- field: bfloat16 [16, 256, 512], P('space', None, 'tm')
The draws below stay inside these ranges and needn't reach their ends.
Inputs may be any that keep to these rules, and one draw needn't show every extreme that they name: Each near_boxes[b, j] lies within 2 of b.
All inputs are finite; a program needn't handle non-finite values.
Results may differ from the reference program's by a relative error of at most 0.008.
Values may be sent and summed in bfloat16 or wider, within the bound.
A program may use at most 192 MiB of HBM per device.

```python
import jax
import jax.numpy as jnp
from jax import lax

R = 256
OFFSETS = 12
NEAR = 8
REACH = 2
TB = 128
BOXES = 16
SAMPLES = 512
N_TM = 4


def draw_near_boxes(key, part):
    boxes = jnp.arange(BOXES, dtype=jnp.int32)[:, None]
    moves = jax.random.randint(jax.random.fold_in(key, 17), (BOXES, NEAR), -REACH, REACH + 1, dtype=jnp.int32)
    return jnp.clip(boxes + moves, 0, BOXES - 1).astype(jnp.int32)


def plant(entries, rng, smallest, largest):
    longest = entries.shape.index(max(entries.shape))
    spots = []
    for shift in (0, 1):
        where = [jax.random.randint(jax.random.fold_in(rng, axis), (), 0, length) for axis, length in enumerate(entries.shape)]
        where[longest] = (where[longest] + shift) % entries.shape[longest]
        spots.append(tuple(where))
    return entries.at[spots[0]].set(smallest).at[spots[1]].set(largest)


def level_of(rng, shape, split, low, high):
    gain, own = 1.0, jax.random.fold_in(rng, 6)
    for position, blocks in split:
        draws = jnp.exp(jax.random.uniform(jax.random.fold_in(own, position), (blocks,), jnp.float32, low / len(split), high / len(split)))
        gain = gain * jnp.repeat(draws, shape[position] // blocks).reshape([-1 if axis == position else 1 for axis in range(len(shape))])
    return gain


def normal_values(stream_key, shape, spread, most, cuts=(), kind=jnp.bfloat16):
    loudness = level_of(stream_key, shape, cuts, -0.22, 0.18) if cuts else 1.0
    entries = jax.random.normal(stream_key, shape, jnp.float32) * spread * loudness
    return jnp.minimum(jnp.maximum(entries, -most), most).astype(kind)


def setup_inputs(seed: int = 0) -> dict:
    arg_keys = jax.random.split(jax.random.key(seed), 6)
    return {
        "signal": normal_values(arg_keys[0], (BOXES, R, SAMPLES), 1.0, 6.0, ((0, 8), (2, 4))),
        "source_boxes": plant(jax.random.randint(arg_keys[1], (BOXES, OFFSETS), 0, BOXES), jax.random.fold_in(arg_keys[1], 1), 0, BOXES - 1).astype(jnp.int32),
        "near_boxes": draw_near_boxes(jax.random.fold_in(arg_keys[5], 71), 0),
        "trans_kernel": normal_values(arg_keys[3], (OFFSETS, R, TB), (OFFSETS * TB) ** -0.5, 0.15625, ((1, 8),), jnp.float32),
        "near_kernel": normal_values(arg_keys[4], (NEAR, TB), (NEAR * TB) ** -0.5, 0.1875, (), jnp.float32),
    }


def block_matrix(kernel):
    width = kernel.shape[-1]
    rows = jnp.arange(2 * width, dtype=jnp.int32)[:, None]
    cols = jnp.arange(width, dtype=jnp.int32)[None, :]
    lagged = cols + width - rows
    valid = (lagged >= 0) & (lagged < width)
    clipped = jnp.clip(lagged, 0, width - 1)
    table = jnp.take(kernel, clipped, axis=-1)
    return jnp.where(valid, table, jnp.zeros_like(table)).astype(jnp.bfloat16)


def reference(signal, source_boxes, near_boxes, trans_kernel, near_kernel):
    blocks = signal.reshape(BOXES, R, N_TM, TB)
    earlier = jnp.concatenate([jnp.zeros_like(blocks[:, :, :1]), blocks[:, :, :-1]], axis=2)
    pair = jnp.concatenate([earlier, blocks], axis=-1)
    pair = jnp.transpose(pair, (1, 0, 2, 3))
    kernels = jnp.transpose(trans_kernel, (1, 0, 2))
    near_mats = block_matrix(near_kernel).astype(jnp.float32)

    def one_ray(inputs):
        rows, kernel = inputs
        trans_mats = block_matrix(kernel).astype(jnp.float32)
        rows32 = rows.astype(jnp.float32)
        far_rows = jnp.take(rows32, source_boxes, axis=0)
        far = jnp.einsum("bkms,kst->bmt", far_rows, trans_mats)
        near_rows = jnp.take(rows32, near_boxes, axis=0)
        near = jnp.einsum("bkms,kst->bmt", near_rows, near_mats)
        return far.astype(jnp.bfloat16), near.astype(jnp.bfloat16)

    far, near = lax.map(one_ray, (pair, kernels))
    field = (far.astype(jnp.float32) + near.astype(jnp.float32)).astype(jnp.bfloat16)
    field = jnp.transpose(field, (1, 0, 2, 3))
    return field.reshape(BOXES, R, SAMPLES)
```

```python
import functools

import jax
import jax.numpy as jnp
import numpy as np
from jax import lax
from jax.experimental import pallas as pl
from jax.experimental.pallas import tpu as pltpu
from jax.sharding import PartitionSpec as P

REACH = 2
MESH = pl.DeviceIdType.MESH
LANES = 128
SUBLANES = 8
def from_behind(shard, axis, by):
    size = lax.axis_size(axis)
    pairs = [(i, i + by) for i in range(size) if 0 <= i + by < size]
    return lax.ppermute(shard, axis, pairs)


def with_halo(block, sides, width):
    for axis, dim in sides:
        count = lax.axis_size(axis)
        forward = [(i, i + 1) for i in range(count - 1)]
        backward = [(target, source) for source, target in forward]
        low = lax.ppermute(
            lax.slice_in_dim(block, block.shape[dim] - width, None, axis=dim), axis, forward
        )
        high = lax.ppermute(lax.slice_in_dim(block, 0, width, axis=dim), axis, backward)
        block = jnp.concatenate([low, block, high], axis=dim)
    return block


def block_matrix(kernel):
    blocklen = kernel.shape[-1]
    leading = kernel.shape[:-1]
    zeroes = jnp.zeros(leading + (2 * blocklen,), jnp.bfloat16)
    widened = jnp.concatenate([zeroes, kernel.astype(jnp.bfloat16)], axis=-1)
    tiled = jnp.tile(widened, (1,) * len(leading) + (2 * blocklen,))
    trimmed = tiled[..., : 2 * blocklen * (3 * blocklen - 1)]
    skewed = trimmed.reshape(leading + (2 * blocklen, 3 * blocklen - 1))
    return skewed[..., :blocklen]


def body(signal, source_boxes, near_boxes, trans_kernel, near_kernel):
    box_dev = signal.shape[0]
    current_rays = lax.all_to_all(signal, "space", split_axis=1, concat_axis=0, tiled=True)
    earlier_rays = from_behind(current_rays, "tm", 1)
    pair_rays = jnp.concatenate([earlier_rays, current_rays], axis=-1)
    offsets = source_boxes.shape[1]
    far = jnp.zeros(current_rays.shape, jnp.float32)
    for offset in range(offsets):
        trans_mats = block_matrix(trans_kernel[offset])
        rows = jnp.take(pair_rays, source_boxes[:, offset], axis=0)
        far = far + jnp.einsum("brs,rst->brt", rows, trans_mats, preferred_element_type=jnp.float32)
    far_rays = far.astype(jnp.bfloat16)
    near_mats = block_matrix(near_kernel)
    slots = near_boxes.shape[1]
    earlier_box = from_behind(signal, "tm", 1)
    pair_box = jnp.concatenate([earlier_box, signal], axis=-1)
    padded = with_halo(pair_box, (("space", 0),), REACH)
    first = lax.axis_index("space") * box_dev
    own_near = lax.dynamic_slice_in_dim(near_boxes, first, box_dev, 0)
    local_rows = own_near - (first - REACH)
    near_sum = jnp.zeros(signal.shape, jnp.float32)
    for slot in range(slots):
        rows = jnp.take(padded, local_rows[:, slot], axis=0)
        near_sum = near_sum + jnp.einsum(
            "brs,st->brt", rows, near_mats[slot], preferred_element_type=jnp.float32
        )
    near_box = near_sum.astype(jnp.bfloat16)
    far_box = lax.all_to_all(far_rays, "space", split_axis=0, concat_axis=1, tiled=True)
    return (far_box.astype(jnp.float32) + near_box.astype(jnp.float32)).astype(jnp.bfloat16)


def spectral_tables(blocklen):
    lags = np.arange(2 * blocklen)[:, None]
    odd = 2 * np.arange(blocklen)[None, :] + 1
    angle = np.pi * lags * odd / (2 * blocklen)
    forward = np.concatenate([np.cos(angle), -np.sin(angle)], axis=1)
    later = angle[blocklen:].T
    inverse = np.concatenate([np.cos(later), -np.sin(later)], axis=0) / blocklen
    return jnp.asarray(forward, jnp.bfloat16), jnp.asarray(inverse, jnp.bfloat16)


def fused_kernel(
    n_tm,
    n_space,
    signal_ref,
    source_ref,
    near_ref,
    trans_ref,
    kernel_ref,
    forward_ref,
    inverse_ref,
    out_ref,
    staged,
    landed,
    spectra,
    responses,
    trans_rows,
    near_rows,
    forward,
    inverse,
    leaving,
    sources,
    nears,
    in_send,
    in_recv,
    out_send,
    out_recv,
    local_sem,
    stage_sem,
):
    tm, space = lax.axis_index("tm"), lax.axis_index("space")
    peers = n_tm * n_space
    box_dev = signal_ref.shape[0]
    boxes = n_space * box_dev
    offsets = trans_ref.shape[0]
    slots = kernel_ref.shape[0]
    rows = n_tm * boxes

    def skipping(position, mine):
        return position + jnp.where(position >= mine, 1, 0)

    mine = space * n_tm + tm
    own_boxes = pl.ds(space * box_dev, box_dev)
    others = []
    for position in range(peers - 1):
        peer = skipping(position, mine)
        others.append((peer % n_tm, peer // n_tm))

    first_ray = pl.multiple_of(tm * SUBLANES, SUBLANES)
    fetches = [
        pltpu.make_async_copy(
            trans_ref.at[:, pl.ds(first_ray, SUBLANES), :], trans_rows, local_sem.at[0]
        ),
        pltpu.make_async_copy(kernel_ref, near_rows, local_sem.at[1]),
        pltpu.make_async_copy(source_ref, sources, local_sem.at[2]),
        pltpu.make_async_copy(near_ref, nears, local_sem.at[3]),
        pltpu.make_async_copy(forward_ref, forward, local_sem.at[4]),
        pltpu.make_async_copy(inverse_ref, inverse, local_sem.at[5]),
    ]
    stagings = [
        pltpu.make_async_copy(signal_ref.at[nth], staged.at[:, nth], stage_sem.at[nth])
        for nth in range(box_dev)
    ]
    for fetch in stagings:
        fetch.start()
    barrier = pltpu.get_barrier_semaphore()
    for other in others:
        pl.semaphore_signal(barrier, inc=1, device_id=other, device_id_type=MESH)
    for fetch in fetches:
        fetch.start()
    pltpu.make_async_copy(signal_ref.at[:, mine], landed.at[tm + 1, own_boxes], in_recv).start()
    for staging in stagings:
        staging.wait()
    pl.semaphore_wait(barrier, peers - 1)
    for other in reversed(others):
        pltpu.make_async_remote_copy(
            src_ref=staged.at[other[1] * n_tm + other[0]],
            dst_ref=landed.at[tm + 1, own_boxes],
            send_sem=in_send,
            recv_sem=in_recv,
            device_id=other,
            device_id_type=MESH,
        ).start()

    for fetch in fetches:
        fetch.wait()

    def respond(lags):
        return jnp.dot(
            lags.astype(jnp.bfloat16), forward[0:LANES, :], preferred_element_type=jnp.float32
        )

    far_real = respond(trans_rows[...].reshape(offsets * SUBLANES, LANES))
    near_real = respond(near_rows[...])
    for entry in range(offsets + slots):
        if entry < offsets:
            both = far_real[entry * SUBLANES : (entry + 1) * SUBLANES, :]
        else:
            slot = entry - offsets
            both = jnp.broadcast_to(near_real[slot : slot + 1, :], (SUBLANES, 2 * LANES))
        real, imag = both[:, :LANES], both[:, LANES:]
        responses[entry, 0] = real
        responses[entry, 1] = imag - real
        responses[entry, 2] = imag + real
    landed[0] = jnp.zeros(landed.shape[1:], jnp.bfloat16)

    arrived = landed.at[pl.ds(1, n_tm)]
    pltpu.make_async_copy(arrived, arrived, in_recv).wait()

    flat = landed[...].astype(jnp.float32).reshape((rows + boxes) * SUBLANES, LANES)
    flat = flat.astype(jnp.bfloat16)
    pair = jnp.concatenate([flat[: rows * SUBLANES], flat[boxes * SUBLANES :]], axis=1)
    both = jnp.dot(pair, forward[...], preferred_element_type=jnp.float32)
    real = both[:, :LANES].reshape(rows, SUBLANES, LANES)
    imag = both[:, LANES:].reshape(rows, SUBLANES, LANES)
    spectra[0] = real
    spectra[1] = imag
    spectra[2] = real + imag

    def finish(to_space):
        wanted = [(nth, block) for nth in range(box_dev) for block in range(n_tm)]
        sums = {}
        for entry in range(offsets + slots):
            factors = [responses[entry, part] for part in range(3)]
            for nth in range(box_dev):
                box = to_space * box_dev + nth
                origin = sources[box, entry] if entry < offsets else nears[entry - offsets, box]
                for block in range(n_tm):
                    row = origin + block * boxes
                    terms = [
                        factors[0] * spectra[2, row],
                        factors[1] * spectra[0, row],
                        factors[2] * spectra[1, row],
                    ]
                    if entry:
                        terms = [x + y for x, y in zip(sums[nth, block], terms)]
                    sums[nth, block] = terms
        real = jnp.concatenate([sums[w][0] - sums[w][2] for w in wanted], axis=0)
        imag = jnp.concatenate([sums[w][0] + sums[w][1] for w in wanted], axis=0)
        spectrum = jnp.concatenate([real, imag], axis=1).astype(jnp.bfloat16)
        field = jnp.dot(spectrum, inverse[...], preferred_element_type=jnp.float32)
        for place, (nth, block) in enumerate(wanted):
            leaving[block, to_space * box_dev + nth] = field[
                place * SUBLANES : (place + 1) * SUBLANES
            ].astype(jnp.bfloat16)

    def dispatch(to_space, own):
        to_boxes = pl.ds(to_space * box_dev, box_dev)
        for position in range(n_tm - 1 if own else n_tm):
            to_tm = skipping(position, tm) if own else position
            pltpu.make_async_remote_copy(
                src_ref=leaving.at[to_tm, to_boxes],
                dst_ref=out_ref.at[:, mine],
                send_sem=out_send,
                recv_sem=out_recv,
                device_id=(to_tm, to_space),
                device_id_type=MESH,
            ).start()
        if own:
            pltpu.make_async_copy(leaving.at[tm, to_boxes], out_ref.at[:, mine], out_recv).start()

    for position in range(n_space - 1):
        finish(skipping(position, space))
        dispatch(skipping(position, space), False)
    finish(space)
    dispatch(space, True)

    sent = staged.at[pl.ds(0, peers - 1)]
    pltpu.make_async_copy(sent, sent, in_send).wait()
    pltpu.make_async_copy(out_ref, out_ref, out_recv).wait()
    pltpu.make_async_copy(sent, sent, out_send).wait()


def fused_body(signal, source_boxes, near_boxes, trans_kernel, near_kernel):
    n_tm, n_space = lax.axis_size("tm"), lax.axis_size("space")
    peers = n_tm * n_space
    box_dev, rays, samples = signal.shape
    boxes = box_dev * n_space
    offsets, slots = trans_kernel.shape[0], near_kernel.shape[0]
    rows = n_tm * boxes
    grouped = signal.reshape(box_dev, peers, SUBLANES, samples)
    forward, inverse = spectral_tables(samples)
    operands = (
        grouped, source_boxes, near_boxes.T, trans_kernel, near_kernel, forward, inverse
    )
    hbm = pl.BlockSpec(memory_space=pltpu.HBM)
    field = pl.pallas_call(
        functools.partial(fused_kernel, n_tm, n_space),
        out_shape=pltpu.VMEM(grouped.shape, jnp.bfloat16),
        in_specs=[hbm] * len(operands),
        out_specs=pl.BlockSpec(memory_space=pl.ANY),
        scratch_shapes=[
            pltpu.VMEM((peers, box_dev, SUBLANES, LANES), jnp.bfloat16),
            pltpu.VMEM((n_tm + 1, boxes, SUBLANES, LANES), jnp.bfloat16),
            pltpu.VMEM((3, rows, SUBLANES, LANES), jnp.float32),
            pltpu.VMEM((offsets + slots, 3, SUBLANES, LANES), jnp.float32),
            pltpu.VMEM((offsets, SUBLANES, LANES), jnp.float32),
            pltpu.VMEM((slots, LANES), jnp.float32),
            pltpu.VMEM(forward.shape, jnp.bfloat16),
            pltpu.VMEM(inverse.shape, jnp.bfloat16),
            pltpu.VMEM((n_tm, boxes, SUBLANES, LANES), jnp.bfloat16),
            pltpu.SMEM(source_boxes.shape, jnp.int32),
            pltpu.SMEM(near_boxes.shape[::-1], jnp.int32),
            pltpu.SemaphoreType.DMA,
            pltpu.SemaphoreType.DMA,
            pltpu.SemaphoreType.DMA,
            pltpu.SemaphoreType.DMA,
            pltpu.SemaphoreType.DMA((6,)),
            pltpu.SemaphoreType.DMA((box_dev,)),
        ],
        compiler_params=pltpu.CompilerParams(
            collective_id=0, has_side_effects=True, vmem_limit_bytes=60*1024*1024
        ),
    )(*[pltpu.with_memory_space_constraint(x, pltpu.HBM) for x in operands])
    return field.reshape(signal.shape)


def routed(signal, source_boxes, near_boxes, trans_kernel, near_kernel):
    n_tm, n_space = lax.axis_size("tm"), lax.axis_size("space")
    box_dev, rays, samples = signal.shape
    rows = n_tm * n_space * box_dev
    fits = rays == n_tm * n_space * SUBLANES and samples == LANES and rows <= 2 * LANES
    chosen = fused_body if fits else body
    return chosen(signal, source_boxes, near_boxes, trans_kernel, near_kernel)


def solution(mesh):
    in_specs = (P("space", None, "tm"), P(), P(), P(None, "space", None), P())
    out_specs = P("space", None, "tm")
    return jax.shard_map(
        routed, mesh=mesh, in_specs=in_specs, out_specs=out_specs, check_vma=False
    )
```

```python
import functools

import jax
import jax.numpy as jnp
import numpy as np
from jax import lax
from jax.experimental import pallas as pl
from jax.experimental.pallas import tpu as pltpu
from jax.sharding import PartitionSpec as P

REACH = 2
MESH = pl.DeviceIdType.MESH
LANES = 128
SUBLANES = 8
def from_behind(shard, axis, by):
    size = lax.axis_size(axis)
    pairs = [(i, i + by) for i in range(size) if 0 <= i + by < size]
    return lax.ppermute(shard, axis, pairs)


def with_halo(block, sides, width):
    for axis, dim in sides:
        count = lax.axis_size(axis)
        forward = [(i, i + 1) for i in range(count - 1)]
        backward = [(target, source) for source, target in forward]
        low = lax.ppermute(
            lax.slice_in_dim(block, block.shape[dim] - width, None, axis=dim), axis, forward
        )
        high = lax.ppermute(lax.slice_in_dim(block, 0, width, axis=dim), axis, backward)
        block = jnp.concatenate([low, block, high], axis=dim)
    return block


def block_matrix(kernel):
    blocklen = kernel.shape[-1]
    leading = kernel.shape[:-1]
    zeroes = jnp.zeros(leading + (2 * blocklen,), jnp.bfloat16)
    widened = jnp.concatenate([zeroes, kernel.astype(jnp.bfloat16)], axis=-1)
    tiled = jnp.tile(widened, (1,) * len(leading) + (2 * blocklen,))
    trimmed = tiled[..., : 2 * blocklen * (3 * blocklen - 1)]
    skewed = trimmed.reshape(leading + (2 * blocklen, 3 * blocklen - 1))
    return skewed[..., :blocklen]


def body(signal, source_boxes, near_boxes, trans_kernel, near_kernel):
    box_dev = signal.shape[0]
    current_rays = lax.all_to_all(signal, "space", split_axis=1, concat_axis=0, tiled=True)
    earlier_rays = from_behind(current_rays, "tm", 1)
    pair_rays = jnp.concatenate([earlier_rays, current_rays], axis=-1)
    offsets = source_boxes.shape[1]
    far = jnp.zeros(current_rays.shape, jnp.float32)
    for offset in range(offsets):
        trans_mats = block_matrix(trans_kernel[offset])
        rows = jnp.take(pair_rays, source_boxes[:, offset], axis=0)
        far = far + jnp.einsum("brs,rst->brt", rows, trans_mats, preferred_element_type=jnp.float32)
    far_rays = far.astype(jnp.bfloat16)
    near_mats = block_matrix(near_kernel)
    slots = near_boxes.shape[1]
    earlier_box = from_behind(signal, "tm", 1)
    pair_box = jnp.concatenate([earlier_box, signal], axis=-1)
    padded = with_halo(pair_box, (("space", 0),), REACH)
    first = lax.axis_index("space") * box_dev
    own_near = lax.dynamic_slice_in_dim(near_boxes, first, box_dev, 0)
    local_rows = own_near - (first - REACH)
    near_sum = jnp.zeros(signal.shape, jnp.float32)
    for slot in range(slots):
        rows = jnp.take(padded, local_rows[:, slot], axis=0)
        near_sum = near_sum + jnp.einsum(
            "brs,st->brt", rows, near_mats[slot], preferred_element_type=jnp.float32
        )
    near_box = near_sum.astype(jnp.bfloat16)
    far_box = lax.all_to_all(far_rays, "space", split_axis=0, concat_axis=1, tiled=True)
    return (far_box.astype(jnp.float32) + near_box.astype(jnp.float32)).astype(jnp.bfloat16)


def spectral_tables(blocklen):
    lags = np.arange(2 * blocklen)[:, None]
    odd = 2 * np.arange(blocklen)[None, :] + 1
    angle = np.pi * lags * odd / (2 * blocklen)
    forward = np.concatenate([np.cos(angle), -np.sin(angle)], axis=1)
    later = angle[blocklen:].T
    inverse = np.concatenate([np.cos(later), -np.sin(later)], axis=0) / blocklen
    return jnp.asarray(forward, jnp.bfloat16), jnp.asarray(inverse, jnp.bfloat16)


def fused_kernel(
    n_tm,
    n_space,
    signal_ref,
    source_ref,
    near_ref,
    trans_ref,
    kernel_ref,
    forward_ref,
    inverse_ref,
    out_ref,
    staged,
    landed,
    spectra,
    responses,
    trans_rows,
    near_rows,
    forward,
    inverse,
    leaving,
    sources,
    nears,
    in_send,
    in_recv,
    out_send,
    out_recv,
    local_sem,
    stage_sem,
):
    tm, space = lax.axis_index("tm"), lax.axis_index("space")
    peers = n_tm * n_space
    box_dev = signal_ref.shape[0]
    boxes = n_space * box_dev
    offsets = trans_ref.shape[0]
    slots = kernel_ref.shape[0]
    rows = n_tm * boxes

    def skipping(position, mine):
        return position + jnp.where(position >= mine, 1, 0)

    mine = space * n_tm + tm
    own_boxes = pl.ds(space * box_dev, box_dev)

    first_ray = pl.multiple_of(tm * SUBLANES, SUBLANES)
    fetches = [
        pltpu.make_async_copy(
            trans_ref.at[:, pl.ds(first_ray, SUBLANES), :], trans_rows, local_sem.at[0]
        ),
        pltpu.make_async_copy(kernel_ref, near_rows, local_sem.at[1]),
        pltpu.make_async_copy(source_ref, sources, local_sem.at[2]),
        pltpu.make_async_copy(near_ref, nears, local_sem.at[3]),
        pltpu.make_async_copy(forward_ref, forward, local_sem.at[4]),
        pltpu.make_async_copy(inverse_ref, inverse, local_sem.at[5]),
    ]
    stagings = [
        pltpu.make_async_copy(signal_ref.at[nth], staged.at[:, nth], stage_sem.at[nth])
        for nth in range(box_dev)
    ]
    barrier = pltpu.get_barrier_semaphore()
    for peer in range(peers):
        to = (peer % n_tm, peer // n_tm)
        pl.semaphore_signal(barrier, inc=1, device_id=to, device_id_type=MESH)
    for fetch in stagings:
        fetch.start()
    for fetch in fetches:
        fetch.start()
    pltpu.make_async_copy(
        signal_ref.at[:, mine], landed.at[tm + 1, own_boxes], in_recv.at[tm]
    ).start()
    for staging in stagings:
        staging.wait()
    pl.semaphore_wait(barrier, peers)
    for position in reversed(range(peers - 1)):
        peer = skipping(position, mine)
        pltpu.make_async_remote_copy(
            src_ref=staged.at[peer],
            dst_ref=landed.at[tm + 1, own_boxes],
            send_sem=in_send,
            recv_sem=in_recv.at[tm],
            device_id=(peer % n_tm, peer // n_tm),
            device_id_type=MESH,
        ).start()

    for fetch in fetches:
        fetch.wait()

    def respond(lags):
        return jnp.dot(
            lags.astype(jnp.bfloat16), forward[0:LANES, :], preferred_element_type=jnp.float32
        )

    far_real = respond(trans_rows[...].reshape(offsets * SUBLANES, LANES))
    near_real = respond(near_rows[...])
    for entry in range(offsets + slots):
        if entry < offsets:
            both = far_real[entry * SUBLANES : (entry + 1) * SUBLANES, :]
        else:
            slot = entry - offsets
            both = jnp.broadcast_to(near_real[slot : slot + 1, :], (SUBLANES, 2 * LANES))
        responses[entry, 0] = both[:, :LANES]
        responses[entry, 1] = both[:, LANES:]
    landed[0] = jnp.zeros(landed.shape[1:], jnp.bfloat16)

    def unpacked(block):
        flat = landed[block].astype(jnp.float32).reshape(boxes * SUBLANES, LANES)
        return flat.astype(jnp.bfloat16)

    for block in reversed(range(n_tm)):
        for arriving in range(block, block - 2, -1):
            if arriving >= 0 and (arriving < block or block == n_tm - 1):
                arrived = landed.at[arriving + 1]
                pltpu.make_async_copy(arrived, arrived, in_recv.at[arriving]).wait()
        pair = jnp.concatenate([unpacked(block), unpacked(block + 1)], axis=1)
        both = jnp.dot(pair, forward[...], preferred_element_type=jnp.float32)
        these = pl.ds(block * boxes, boxes)
        spectra[0, these] = both[:, :LANES].reshape(boxes, SUBLANES, LANES)
        spectra[1, these] = both[:, LANES:].reshape(boxes, SUBLANES, LANES)

    def finish(to_space):
        wanted = [(nth, block) for nth in range(box_dev) for block in range(n_tm)]
        reals, imags = {}, {}
        for entry in range(offsets + slots):
            c, d = responses[entry, 0], responses[entry, 1]
            for nth in range(box_dev):
                box = to_space * box_dev + nth
                origin = sources[box, entry] if entry < offsets else nears[entry - offsets, box]
                for block in range(n_tm):
                    a, b = (spectra[part, origin + block * boxes] for part in range(2))
                    real, imag = a * c - b * d, a * d + b * c
                    if entry:
                        real, imag = reals[nth, block] + real, imags[nth, block] + imag
                    reals[nth, block], imags[nth, block] = real, imag
        real = jnp.concatenate([reals[w] for w in wanted], axis=0)
        imag = jnp.concatenate([imags[w] for w in wanted], axis=0)
        spectrum = jnp.concatenate([real, imag], axis=1).astype(jnp.bfloat16)
        field = jnp.dot(spectrum, inverse[...], preferred_element_type=jnp.float32)
        for place, (nth, block) in enumerate(wanted):
            leaving[block, to_space * box_dev + nth] = field[
                place * SUBLANES : (place + 1) * SUBLANES
            ].astype(jnp.bfloat16)

    def dispatch(to_space):
        to_boxes = pl.ds(to_space * box_dev, box_dev)

        def remote(to_tm):
            pltpu.make_async_remote_copy(
                src_ref=leaving.at[to_tm, to_boxes],
                dst_ref=out_ref.at[:, mine],
                send_sem=out_send,
                recv_sem=out_recv,
                device_id=(to_tm, to_space),
                device_id_type=MESH,
            ).start()

        for position in range(n_tm - 1):
            remote(skipping(position, tm))

        @pl.when(space != to_space)
        def _():
            remote(tm)

        @pl.when(space == to_space)
        def _():
            pltpu.make_async_copy(leaving.at[tm, to_boxes], out_ref.at[:, mine], out_recv).start()

    def serve(to_space, carry):
        finish(to_space)
        dispatch(to_space)
        return carry

    lax.fori_loop(0, n_space, serve, 0)

    sent = staged.at[pl.ds(0, peers - 1)]
    pltpu.make_async_copy(sent, sent, in_send).wait()
    pltpu.make_async_copy(out_ref, out_ref, out_recv).wait()
    pltpu.make_async_copy(sent, sent, out_send).wait()


def fused_body(signal, source_boxes, near_boxes, trans_kernel, near_kernel):
    n_tm, n_space = lax.axis_size("tm"), lax.axis_size("space")
    peers = n_tm * n_space
    box_dev, rays, samples = signal.shape
    boxes = box_dev * n_space
    offsets, slots = trans_kernel.shape[0], near_kernel.shape[0]
    rows = n_tm * boxes
    grouped = signal.reshape(box_dev, peers, SUBLANES, samples)
    forward, inverse = spectral_tables(samples)
    operands = (
        grouped, source_boxes, near_boxes.T, trans_kernel, near_kernel, forward, inverse
    )
    hbm = pl.BlockSpec(memory_space=pltpu.HBM)
    field = pl.pallas_call(
        functools.partial(fused_kernel, n_tm, n_space),
        out_shape=pltpu.VMEM(grouped.shape, jnp.bfloat16),
        in_specs=[hbm] * len(operands),
        out_specs=pl.BlockSpec(memory_space=pl.ANY),
        scratch_shapes=[
            pltpu.VMEM((peers, box_dev, SUBLANES, LANES), jnp.bfloat16),
            pltpu.VMEM((n_tm + 1, boxes, SUBLANES, LANES), jnp.bfloat16),
            pltpu.VMEM((2, rows, SUBLANES, LANES), jnp.float32),
            pltpu.VMEM((offsets + slots, 2, SUBLANES, LANES), jnp.float32),
            pltpu.VMEM((offsets, SUBLANES, LANES), jnp.float32),
            pltpu.VMEM((slots, LANES), jnp.float32),
            pltpu.VMEM(forward.shape, jnp.bfloat16),
            pltpu.VMEM(inverse.shape, jnp.bfloat16),
            pltpu.VMEM((n_tm, boxes, SUBLANES, LANES), jnp.bfloat16),
            pltpu.SMEM(source_boxes.shape, jnp.int32),
            pltpu.SMEM(near_boxes.shape[::-1], jnp.int32),
            pltpu.SemaphoreType.DMA,
            pltpu.SemaphoreType.DMA((n_tm,)),
            pltpu.SemaphoreType.DMA,
            pltpu.SemaphoreType.DMA,
            pltpu.SemaphoreType.DMA((6,)),
            pltpu.SemaphoreType.DMA((box_dev,)),
        ],
        compiler_params=pltpu.CompilerParams(
            collective_id=0, has_side_effects=True, vmem_limit_bytes=60*1024*1024
        ),
    )(*[pltpu.with_memory_space_constraint(x, pltpu.HBM) for x in operands])
    return field.reshape(signal.shape)


def routed(signal, source_boxes, near_boxes, trans_kernel, near_kernel):
    n_tm, n_space = lax.axis_size("tm"), lax.axis_size("space")
    box_dev, rays, samples = signal.shape
    rows = n_tm * n_space * box_dev
    fits = rays == n_tm * n_space * SUBLANES and samples == LANES and rows <= 2 * LANES
    chosen = fused_body if fits else body
    return chosen(signal, source_boxes, near_boxes, trans_kernel, near_kernel)


def solution(mesh):
    in_specs = (P("space", None, "tm"), P(), P(), P(None, "space", None), P())
    out_specs = P("space", None, "tm")
    return jax.shard_map(
        routed, mesh=mesh, in_specs=in_specs, out_specs=out_specs, check_vma=False
    )
```

```python
import functools

import jax
import jax.numpy as jnp
import numpy as np
from jax import lax
from jax.experimental import pallas as pl
from jax.experimental.pallas import tpu as pltpu
from jax.sharding import PartitionSpec as P

REACH = 2
MESH = pl.DeviceIdType.MESH
LANES = 128
SUBLANES = 8
def from_behind(shard, axis, by):
    size = lax.axis_size(axis)
    pairs = [(i, i + by) for i in range(size) if 0 <= i + by < size]
    return lax.ppermute(shard, axis, pairs)


def with_halo(block, sides, width):
    for axis, dim in sides:
        count = lax.axis_size(axis)
        forward = [(i, i + 1) for i in range(count - 1)]
        backward = [(target, source) for source, target in forward]
        low = lax.ppermute(
            lax.slice_in_dim(block, block.shape[dim] - width, None, axis=dim), axis, forward
        )
        high = lax.ppermute(lax.slice_in_dim(block, 0, width, axis=dim), axis, backward)
        block = jnp.concatenate([low, block, high], axis=dim)
    return block


def block_matrix(kernel):
    blocklen = kernel.shape[-1]
    leading = kernel.shape[:-1]
    zeroes = jnp.zeros(leading + (2 * blocklen,), jnp.bfloat16)
    widened = jnp.concatenate([zeroes, kernel.astype(jnp.bfloat16)], axis=-1)
    tiled = jnp.tile(widened, (1,) * len(leading) + (2 * blocklen,))
    trimmed = tiled[..., : 2 * blocklen * (3 * blocklen - 1)]
    skewed = trimmed.reshape(leading + (2 * blocklen, 3 * blocklen - 1))
    return skewed[..., :blocklen]


def body(signal, source_boxes, near_boxes, trans_kernel, near_kernel):
    box_dev = signal.shape[0]
    current_rays = lax.all_to_all(signal, "space", split_axis=1, concat_axis=0, tiled=True)
    earlier_rays = from_behind(current_rays, "tm", 1)
    pair_rays = jnp.concatenate([earlier_rays, current_rays], axis=-1)
    offsets = source_boxes.shape[1]
    far = jnp.zeros(current_rays.shape, jnp.float32)
    for offset in range(offsets):
        trans_mats = block_matrix(trans_kernel[offset])
        rows = jnp.take(pair_rays, source_boxes[:, offset], axis=0)
        far = far + jnp.einsum("brs,rst->brt", rows, trans_mats, preferred_element_type=jnp.float32)
    far_rays = far.astype(jnp.bfloat16)
    near_mats = block_matrix(near_kernel)
    slots = near_boxes.shape[1]
    earlier_box = from_behind(signal, "tm", 1)
    pair_box = jnp.concatenate([earlier_box, signal], axis=-1)
    padded = with_halo(pair_box, (("space", 0),), REACH)
    first = lax.axis_index("space") * box_dev
    own_near = lax.dynamic_slice_in_dim(near_boxes, first, box_dev, 0)
    local_rows = own_near - (first - REACH)
    near_sum = jnp.zeros(signal.shape, jnp.float32)
    for slot in range(slots):
        rows = jnp.take(padded, local_rows[:, slot], axis=0)
        near_sum = near_sum + jnp.einsum(
            "brs,st->brt", rows, near_mats[slot], preferred_element_type=jnp.float32
        )
    near_box = near_sum.astype(jnp.bfloat16)
    far_box = lax.all_to_all(far_rays, "space", split_axis=0, concat_axis=1, tiled=True)
    return (far_box.astype(jnp.float32) + near_box.astype(jnp.float32)).astype(jnp.bfloat16)


def spectral_tables(blocklen):
    lags = np.arange(2 * blocklen)[:, None]
    odd = 2 * np.arange(blocklen)[None, :] + 1
    angle = np.pi * lags * odd / (2 * blocklen)
    forward = np.concatenate([np.cos(angle), -np.sin(angle)], axis=1)
    later = angle[blocklen:].T
    inverse = np.concatenate([np.cos(later), -np.sin(later)], axis=0) / blocklen
    return jnp.asarray(forward, jnp.bfloat16), jnp.asarray(inverse, jnp.bfloat16)


def fused_kernel(
    n_tm,
    n_space,
    signal_ref,
    source_ref,
    near_ref,
    trans_ref,
    kernel_ref,
    forward_ref,
    inverse_ref,
    out_ref,
    staged,
    landed,
    spectra,
    responses,
    trans_rows,
    near_rows,
    forward,
    inverse,
    leaving,
    sources,
    nears,
    in_send,
    in_recv,
    out_send,
    out_recv,
    local_sem,
    stage_sem,
):
    tm, space = lax.axis_index("tm"), lax.axis_index("space")
    peers = n_tm * n_space
    box_dev = signal_ref.shape[0]
    boxes = n_space * box_dev
    offsets = trans_ref.shape[0]
    slots = kernel_ref.shape[0]
    rows = n_tm * boxes

    def skipping(position, mine):
        return position + jnp.where(position >= mine, 1, 0)

    mine = space * n_tm + tm
    own_boxes = pl.ds(space * box_dev, box_dev)

    first_ray = pl.multiple_of(tm * SUBLANES, SUBLANES)
    fetches = [
        pltpu.make_async_copy(
            trans_ref.at[:, pl.ds(first_ray, SUBLANES), :], trans_rows, local_sem.at[0]
        ),
        pltpu.make_async_copy(kernel_ref, near_rows, local_sem.at[1]),
        pltpu.make_async_copy(source_ref, sources, local_sem.at[2]),
        pltpu.make_async_copy(near_ref, nears, local_sem.at[3]),
        pltpu.make_async_copy(forward_ref, forward, local_sem.at[4]),
        pltpu.make_async_copy(inverse_ref, inverse, local_sem.at[5]),
    ]
    stagings = [
        pltpu.make_async_copy(signal_ref.at[nth], staged.at[:, nth], stage_sem.at[nth])
        for nth in range(box_dev)
    ]
    barrier = pltpu.get_barrier_semaphore()
    for peer in range(peers):
        to = (peer % n_tm, peer // n_tm)
        pl.semaphore_signal(barrier, inc=1, device_id=to, device_id_type=MESH)
    for fetch in stagings:
        fetch.start()
    for fetch in fetches:
        fetch.start()
    pltpu.make_async_copy(
        signal_ref.at[:, mine], landed.at[tm + 1, own_boxes], in_recv.at[tm]
    ).start()
    for staging in stagings:
        staging.wait()
    pl.semaphore_wait(barrier, peers)
    for position in reversed(range(peers - 1)):
        peer = skipping(position, mine)
        pltpu.make_async_remote_copy(
            src_ref=staged.at[peer],
            dst_ref=landed.at[tm + 1, own_boxes],
            send_sem=in_send,
            recv_sem=in_recv.at[tm],
            device_id=(peer % n_tm, peer // n_tm),
            device_id_type=MESH,
        ).start()

    for fetch in fetches:
        fetch.wait()

    def respond(lags):
        return jnp.dot(
            lags.astype(jnp.bfloat16), forward[0:LANES, :], preferred_element_type=jnp.float32
        )

    far_real = respond(trans_rows[...].reshape(offsets * SUBLANES, LANES))
    near_real = respond(near_rows[...])
    for entry in range(offsets + slots):
        if entry < offsets:
            both = far_real[entry * SUBLANES : (entry + 1) * SUBLANES, :]
        else:
            slot = entry - offsets
            both = jnp.broadcast_to(near_real[slot : slot + 1, :], (SUBLANES, 2 * LANES))
        real, imag = both[:, :LANES], both[:, LANES:]
        responses[entry, 0] = real
        responses[entry, 1] = imag - real
        responses[entry, 2] = imag + real
    landed[0] = jnp.zeros(landed.shape[1:], jnp.bfloat16)

    def unpacked(block):
        flat = landed[block].astype(jnp.float32).reshape(boxes * SUBLANES, LANES)
        return flat.astype(jnp.bfloat16)

    for block in reversed(range(n_tm)):
        for arriving in range(block, block - 2, -1):
            if arriving >= 0 and (arriving < block or block == n_tm - 1):
                arrived = landed.at[arriving + 1]
                pltpu.make_async_copy(arrived, arrived, in_recv.at[arriving]).wait()
        pair = jnp.concatenate([unpacked(block), unpacked(block + 1)], axis=1)
        both = jnp.dot(pair, forward[...], preferred_element_type=jnp.float32)
        spectra[:, 2 * block] = both[:, :LANES].reshape(boxes, SUBLANES, LANES)
        spectra[:, 2 * block + 1] = both[:, LANES:].reshape(boxes, SUBLANES, LANES)

    def finish(to_space):
        wanted = [(nth, block) for nth in range(box_dev) for block in range(n_tm)]
        sums = {}
        for entry in range(offsets + slots):
            factors = [responses[entry, part] for part in range(3)]
            for nth in range(box_dev):
                box = to_space * box_dev + nth
                origin = sources[box, entry] if entry < offsets else nears[entry - offsets, box]
                for block in range(n_tm):
                    a, b = (spectra[origin, 2 * block + part] for part in range(2))
                    terms = [factors[0] * (a + b), factors[1] * a, factors[2] * b]
                    if entry:
                        terms = [x + y for x, y in zip(sums[nth, block], terms)]
                    sums[nth, block] = terms
        real = jnp.concatenate([sums[w][0] - sums[w][2] for w in wanted], axis=0)
        imag = jnp.concatenate([sums[w][0] + sums[w][1] for w in wanted], axis=0)
        spectrum = jnp.concatenate([real, imag], axis=1).astype(jnp.bfloat16)
        field = jnp.dot(spectrum, inverse[...], preferred_element_type=jnp.float32)
        for place, (nth, block) in enumerate(wanted):
            leaving[block, to_space * box_dev + nth] = field[
                place * SUBLANES : (place + 1) * SUBLANES
            ].astype(jnp.bfloat16)

    def dispatch(to_space):
        to_boxes = pl.ds(to_space * box_dev, box_dev)

        def remote(to_tm):
            pltpu.make_async_remote_copy(
                src_ref=leaving.at[to_tm, to_boxes],
                dst_ref=out_ref.at[:, mine],
                send_sem=out_send,
                recv_sem=out_recv,
                device_id=(to_tm, to_space),
                device_id_type=MESH,
            ).start()

        for position in range(n_tm - 1):
            remote(skipping(position, tm))

        @pl.when(space != to_space)
        def _():
            remote(tm)

        @pl.when(space == to_space)
        def _():
            pltpu.make_async_copy(leaving.at[tm, to_boxes], out_ref.at[:, mine], out_recv).start()

    def serve(to_space, carry):
        finish(to_space)
        dispatch(to_space)
        return carry

    lax.fori_loop(0, n_space, serve, 0)

    sent = staged.at[pl.ds(0, peers - 1)]
    pltpu.make_async_copy(sent, sent, in_send).wait()
    pltpu.make_async_copy(out_ref, out_ref, out_recv).wait()
    pltpu.make_async_copy(sent, sent, out_send).wait()


def fused_body(signal, source_boxes, near_boxes, trans_kernel, near_kernel):
    n_tm, n_space = lax.axis_size("tm"), lax.axis_size("space")
    peers = n_tm * n_space
    box_dev, rays, samples = signal.shape
    boxes = box_dev * n_space
    offsets, slots = trans_kernel.shape[0], near_kernel.shape[0]
    rows = n_tm * boxes
    grouped = signal.reshape(box_dev, peers, SUBLANES, samples)
    forward, inverse = spectral_tables(samples)
    operands = (
        grouped, source_boxes, near_boxes.T, trans_kernel, near_kernel, forward, inverse
    )
    hbm = pl.BlockSpec(memory_space=pltpu.HBM)
    field = pl.pallas_call(
        functools.partial(fused_kernel, n_tm, n_space),
        out_shape=pltpu.VMEM(grouped.shape, jnp.bfloat16),
        in_specs=[hbm] * len(operands),
        out_specs=pl.BlockSpec(memory_space=pl.ANY),
        scratch_shapes=[
            pltpu.VMEM((peers, box_dev, SUBLANES, LANES), jnp.bfloat16),
            pltpu.VMEM((n_tm + 1, boxes, SUBLANES, LANES), jnp.bfloat16),
            pltpu.VMEM((boxes, 2 * n_tm, SUBLANES, LANES), jnp.float32),
            pltpu.VMEM((offsets + slots, 3, SUBLANES, LANES), jnp.float32),
            pltpu.VMEM((offsets, SUBLANES, LANES), jnp.float32),
            pltpu.VMEM((slots, LANES), jnp.float32),
            pltpu.VMEM(forward.shape, jnp.bfloat16),
            pltpu.VMEM(inverse.shape, jnp.bfloat16),
            pltpu.VMEM((n_tm, boxes, SUBLANES, LANES), jnp.bfloat16),
            pltpu.SMEM(source_boxes.shape, jnp.int32),
            pltpu.SMEM(near_boxes.shape[::-1], jnp.int32),
            pltpu.SemaphoreType.DMA,
            pltpu.SemaphoreType.DMA((n_tm,)),
            pltpu.SemaphoreType.DMA,
            pltpu.SemaphoreType.DMA,
            pltpu.SemaphoreType.DMA((6,)),
            pltpu.SemaphoreType.DMA((box_dev,)),
        ],
        compiler_params=pltpu.CompilerParams(
            collective_id=0, has_side_effects=True, vmem_limit_bytes=60*1024*1024
        ),
    )(*[pltpu.with_memory_space_constraint(x, pltpu.HBM) for x in operands])
    return field.reshape(signal.shape)


def routed(signal, source_boxes, near_boxes, trans_kernel, near_kernel):
    n_tm, n_space = lax.axis_size("tm"), lax.axis_size("space")
    box_dev, rays, samples = signal.shape
    rows = n_tm * n_space * box_dev
    fits = rays == n_tm * n_space * SUBLANES and samples == LANES and rows <= 2 * LANES
    chosen = fused_body if fits else body
    return chosen(signal, source_boxes, near_boxes, trans_kernel, near_kernel)


def solution(mesh):
    in_specs = (P("space", None, "tm"), P(), P(), P(None, "space", None), P())
    out_specs = P("space", None, "tm")
    return jax.shard_map(
        routed, mesh=mesh, in_specs=in_specs, out_specs=out_specs, check_vma=False
    )
```

```python
import functools

import jax
import jax.numpy as jnp
import numpy as np
from jax import lax
from jax.experimental import pallas as pl
from jax.experimental.pallas import tpu as pltpu
from jax.sharding import PartitionSpec as P

REACH = 2
MESH = pl.DeviceIdType.MESH
LANES = 128
SUBLANES = 8
SHARE = 4
ORDERS = ((0,3,1,2),(0,1,2,3),(0,1,2,3),(1,0,2,3))
def from_behind(shard, axis, by):
    size = lax.axis_size(axis)
    pairs = [(i, i + by) for i in range(size) if 0 <= i + by < size]
    return lax.ppermute(shard, axis, pairs)


def with_halo(block, sides, width):
    for axis, dim in sides:
        count = lax.axis_size(axis)
        forward = [(i, i + 1) for i in range(count - 1)]
        backward = [(target, source) for source, target in forward]
        low = lax.ppermute(
            lax.slice_in_dim(block, block.shape[dim] - width, None, axis=dim), axis, forward
        )
        high = lax.ppermute(lax.slice_in_dim(block, 0, width, axis=dim), axis, backward)
        block = jnp.concatenate([low, block, high], axis=dim)
    return block


def block_matrix(kernel):
    blocklen = kernel.shape[-1]
    leading = kernel.shape[:-1]
    zeroes = jnp.zeros(leading + (2 * blocklen,), jnp.bfloat16)
    widened = jnp.concatenate([zeroes, kernel.astype(jnp.bfloat16)], axis=-1)
    tiled = jnp.tile(widened, (1,) * len(leading) + (2 * blocklen,))
    trimmed = tiled[..., : 2 * blocklen * (3 * blocklen - 1)]
    skewed = trimmed.reshape(leading + (2 * blocklen, 3 * blocklen - 1))
    return skewed[..., :blocklen]


def body(signal, source_boxes, near_boxes, trans_kernel, near_kernel):
    box_dev = signal.shape[0]
    current_rays = lax.all_to_all(signal, "space", split_axis=1, concat_axis=0, tiled=True)
    earlier_rays = from_behind(current_rays, "tm", 1)
    pair_rays = jnp.concatenate([earlier_rays, current_rays], axis=-1)
    offsets = source_boxes.shape[1]
    far = jnp.zeros(current_rays.shape, jnp.float32)
    for offset in range(offsets):
        trans_mats = block_matrix(trans_kernel[offset])
        rows = jnp.take(pair_rays, source_boxes[:, offset], axis=0)
        far = far + jnp.einsum("brs,rst->brt", rows, trans_mats, preferred_element_type=jnp.float32)
    far_rays = far.astype(jnp.bfloat16)
    near_mats = block_matrix(near_kernel)
    slots = near_boxes.shape[1]
    earlier_box = from_behind(signal, "tm", 1)
    pair_box = jnp.concatenate([earlier_box, signal], axis=-1)
    padded = with_halo(pair_box, (("space", 0),), REACH)
    first = lax.axis_index("space") * box_dev
    own_near = lax.dynamic_slice_in_dim(near_boxes, first, box_dev, 0)
    local_rows = own_near - (first - REACH)
    near_sum = jnp.zeros(signal.shape, jnp.float32)
    for slot in range(slots):
        rows = jnp.take(padded, local_rows[:, slot], axis=0)
        near_sum = near_sum + jnp.einsum(
            "brs,st->brt", rows, near_mats[slot], preferred_element_type=jnp.float32
        )
    near_box = near_sum.astype(jnp.bfloat16)
    far_box = lax.all_to_all(far_rays, "space", split_axis=0, concat_axis=1, tiled=True)
    return (far_box.astype(jnp.float32) + near_box.astype(jnp.float32)).astype(jnp.bfloat16)


def spectral_tables(blocklen):
    lags = np.arange(2 * blocklen)[:, None]
    odd = 2 * np.arange(blocklen)[None, :] + 1
    angle = np.pi * lags * odd / (2 * blocklen)
    forward = np.concatenate([np.cos(angle), -np.sin(angle)], axis=1)
    later = angle[blocklen:].T
    inverse = np.concatenate([np.cos(later), -np.sin(later)], axis=0) / blocklen
    return jnp.asarray(forward, jnp.bfloat16), jnp.asarray(inverse, jnp.bfloat16)


def fused_kernel(
    n_tm,
    n_space,
    signal_ref,
    source_ref,
    near_ref,
    trans_ref,
    kernel_ref,
    forward_ref,
    inverse_ref,
    out_ref,
    staged,
    landed,
    spectra,
    responses,
    near_responses,
    trans_rows,
    near_rows,
    forward,
    inverse,
    leaving,
    sources,
    nears,
    in_send,
    in_recv,
    out_send,
    out_recv,
    local_sem,
    stage_sem,
    ready,
):
    tm, space = lax.axis_index("tm"), lax.axis_index("space")
    peers = n_tm * n_space
    last = n_tm - 1
    box_dev = signal_ref.shape[0]
    boxes = n_space * box_dev
    offsets = trans_ref.shape[0]
    slots = kernel_ref.shape[0]
    on_first, on_last = tm == 0, tm == last
    on_edge = jnp.logical_or(on_first, on_last)
    on_middle = jnp.logical_not(on_edge)

    orders = ORDERS
    def awaited(line, turn):
        def needs(item):
            if line in (0, last) and item == last:
                return {0, last + 2} if line else {last + 1}
            shift = 1 if line == last else 0
            return {item + shift, item + 1 + shift} - ({0} if line < last else set())

        before = [needs(item) for item in orders[line][:turn]]
        return sorted(needs(orders[line][turn]).difference(*before))

    def item_at(turn):
        item = orders[0][turn]
        for line in range(1, n_tm):
            item = jnp.where(tm == line, orders[line][turn], item)
        return item

    def swapped(item):
        return jnp.logical_and(on_edge, item == last)

    def group_of(item):
        return jnp.where(swapped(item), last - tm, tm)

    def places(item):
        shift = jnp.where(on_last, 1, 0)
        return jnp.where(swapped(item), 0, item + shift), item + 1 + shift

    def skipping(position, mine):
        return position + jnp.where(position >= mine, 1, 0)

    own_boxes = pl.ds(space * box_dev, box_dev)
    barrier = pltpu.get_barrier_semaphore()

    def greet(to_tm):
        for to_space in range(n_space):
            to = (to_tm, to_space)
            pl.semaphore_signal(barrier, inc=1, device_id=to, device_id_type=MESH)

    @pl.when(tm < last)
    def _():
        greet(0)

    for to_tm in range(1, n_tm):
        greet(to_tm)

    fetches = [
        pltpu.make_async_copy(trans_ref, trans_rows, local_sem.at[0]),
        pltpu.make_async_copy(kernel_ref, near_rows, local_sem.at[1]),
        pltpu.make_async_copy(source_ref, sources, local_sem.at[2]),
        pltpu.make_async_copy(near_ref, nears, local_sem.at[3]),
        pltpu.make_async_copy(forward_ref, forward, local_sem.at[4]),
        pltpu.make_async_copy(inverse_ref, inverse, local_sem.at[5]),
    ]
    stagings = [
        pltpu.make_async_copy(signal_ref.at[nth], staged.at[:, nth], stage_sem.at[nth])
        for nth in range(box_dev)
    ]
    for fetch in stagings + fetches:
        fetch.start()
    for staging in stagings:
        staging.wait()

    def place_of(place):
        return landed.at[place, own_boxes]

    def send_in(to_tm, to_space, group, place):
        pltpu.make_async_remote_copy(
            src_ref=staged.at[to_space * n_tm + group],
            dst_ref=place_of(place),
            send_sem=in_send,
            recv_sem=in_recv.at[place],
            device_id=(to_tm, to_space),
            device_id_type=MESH,
        ).start()

    def keep_in(group, place):
        source = staged.at[space * n_tm + group]
        pltpu.make_async_copy(source, place_of(place), in_recv.at[place]).start()

    @pl.when(on_first)
    def _():
        pl.semaphore_wait(barrier, last * n_space)
        for position in reversed(range(last * n_space - 1)):
            peer = skipping(position, space * last)
            to_tm, to_space = peer % last, peer // last
            send_in(to_tm, to_space, to_tm, 1)
        for position in reversed(range(n_space - 1)):
            send_in(0, skipping(position, space), last, n_tm)
        keep_in(0, 1)
        keep_in(last, n_tm)
        pl.semaphore_wait(ready, n_space)
        for to_space in reversed(range(n_space)):
            send_in(last, to_space, last, 1)

    @pl.when(on_middle)
    def _():
        pl.semaphore_wait(barrier, peers)
        for position in reversed(range(peers - 1)):
            peer = skipping(position, space * n_tm + tm)
            to_tm, to_space = peer % n_tm, peer // n_tm
            send_in(to_tm, to_space, to_tm, tm + 1)
        keep_in(tm, tm + 1)

        @pl.when(tm == last - 1)
        def _():
            for to_space in reversed(range(n_space)):
                send_in(last, to_space, 0, 0)

    @pl.when(on_last)
    def _():
        pl.semaphore_wait(barrier, peers)
        for to_space in range(n_space):
            pl.semaphore_signal(ready, inc=1, device_id=(0, to_space), device_id_type=MESH)
        for position in reversed(range(last * n_space - 1)):
            peer = skipping(position, space * last + last - 1)
            to_tm, to_space = peer % last + 1, peer // last
            send_in(to_tm, to_space, to_tm, n_tm)
        for position in reversed(range(n_space - 1)):
            send_in(last, skipping(position, space), 0, n_tm + 1)
        keep_in(last, n_tm)
        keep_in(0, n_tm + 1)

    for fetch in fetches:
        fetch.wait()

    def respond(lags):
        return jnp.dot(
            lags.astype(jnp.bfloat16), forward[0:LANES, :], preferred_element_type=jnp.float32
        )

    def keep_response(where, both):
        real, imag = both[:, :LANES], both[:, LANES:]
        where[0] = real
        where[1] = imag - real
        where[2] = imag + real

    for turn in range(n_tm):
        first_ray = pl.multiple_of(group_of(item_at(turn)) * SUBLANES, SUBLANES)
        far = respond(
            trans_rows[:, pl.ds(first_ray, SUBLANES), :].reshape(offsets * SUBLANES, LANES)
        )
        for entry in range(offsets):
            these = slice(entry * SUBLANES, (entry + 1) * SUBLANES)
            keep_response(responses.at[turn, entry], far[these])
    near = respond(near_rows[...])
    for slot in range(slots):
        both = jnp.broadcast_to(near[slot : slot + 1, :], (SUBLANES, 2 * LANES))
        keep_response(near_responses.at[slot], both)

    def arrive(place):
        arrived = landed.at[place]
        pltpu.make_async_copy(arrived, arrived, in_recv.at[place]).wait()

    def unpacked(place):
        flat = landed[place].astype(jnp.float32).reshape(boxes * SUBLANES, LANES)
        return flat.astype(jnp.bfloat16)

    def transform(turn):
        earlier, current = places(item_at(turn))
        pair = jnp.concatenate([unpacked(earlier), unpacked(current)], axis=1)
        both = jnp.dot(pair, forward[...], preferred_element_type=jnp.float32)
        spectra[:, 2 * turn] = both[:, :LANES].reshape(boxes, SUBLANES, LANES)
        spectra[:, 2 * turn + 1] = both[:, LANES:].reshape(boxes, SUBLANES, LANES)

    def finish(turn, first):
        targets = [first * box_dev + nth for nth in range(SHARE * box_dev)]
        sums = [None] * len(targets)
        for entry in range(offsets + slots):
            if entry < offsets:
                factors = [responses[turn, entry, part] for part in range(3)]
            else:
                factors = [near_responses[entry - offsets, part] for part in range(3)]
            for place, box in enumerate(targets):
                origin = sources[box, entry] if entry < offsets else nears[entry - offsets, box]
                a, b = (spectra[origin, 2 * turn + part] for part in range(2))
                terms = [factors[0] * (a + b), factors[1] * a, factors[2] * b]
                if entry:
                    terms = [x + y for x, y in zip(sums[place], terms)]
                sums[place] = terms
        real = jnp.concatenate([x - z for x, y, z in sums], axis=0)
        imag = jnp.concatenate([x + y for x, y, z in sums], axis=0)
        spectrum = jnp.concatenate([real, imag], axis=1).astype(jnp.bfloat16)
        field = jnp.dot(spectrum, inverse[...], preferred_element_type=jnp.float32)
        for nth, box in enumerate(targets):
            leaving[turn, box] = field[nth * SUBLANES : (nth + 1) * SUBLANES].astype(jnp.bfloat16)

    def deliver(turn, first):
        item = item_at(turn)
        to_tm = jnp.where(swapped(item), tm, item + jnp.where(on_last, 1, 0))
        target = out_ref.at[:, space * n_tm + group_of(item)]
        own_line = to_tm == tm
        own_here = jnp.logical_and(own_line, space // SHARE == first // SHARE)

        def source(to_space):
            return leaving.at[turn, pl.ds(to_space * box_dev, box_dev)]

        def send_out(to_space):
            pltpu.make_async_remote_copy(
                src_ref=source(to_space),
                dst_ref=target,
                send_sem=out_send,
                recv_sem=out_recv,
                device_id=(to_tm, to_space),
                device_id_type=MESH,
            ).start()

        @pl.when(jnp.logical_not(own_here))
        def _():
            for nth in range(SHARE):
                send_out(first + nth)

        @pl.when(own_here)
        def _():
            for position in range(SHARE - 1):
                send_out(first + skipping(position, space - first))
            pltpu.make_async_copy(source(space), target, out_recv).start()

    @pl.when(tm < last)
    def _():
        landed[0] = jnp.zeros(landed.shape[1:], jnp.bfloat16)

    for turn in range(n_tm):
        for line in range(n_tm):
            if awaited(line, turn):

                @pl.when(tm == line)
                def _():
                    for place in awaited(line, turn):
                        arrive(place)

        transform(turn)

        def serve(part, carry, turn=turn):
            finish(turn, part * SHARE)
            deliver(turn, part * SHARE)
            return carry

        lax.fori_loop(0, n_space // SHARE, serve, 0)

    def settle(pieces, sem):
        sent = staged.at[pl.ds(0, pieces)]
        pltpu.make_async_copy(sent, sent, sem).wait()

    @pl.when(on_first)
    def _():
        settle(last * n_space - 1 + n_space - 1, in_send)
        settle(n_space, in_send)

    @pl.when(on_middle)
    def _():
        settle(peers - 1, in_send)

        @pl.when(tm == last - 1)
        def _():
            settle(n_space, in_send)

    @pl.when(on_last)
    def _():
        settle(last * n_space - 1 + n_space - 1, in_send)

    pltpu.make_async_copy(out_ref, out_ref, out_recv).wait()

    @pl.when(on_middle)
    def _():
        settle(peers - 1, out_send)

    @pl.when(on_edge)
    def _():
        settle(peers - 2, out_send)


def fused_body(signal, source_boxes, near_boxes, trans_kernel, near_kernel):
    n_tm, n_space = lax.axis_size("tm"), lax.axis_size("space")
    peers = n_tm * n_space
    box_dev, rays, samples = signal.shape
    boxes = box_dev * n_space
    offsets, slots = trans_kernel.shape[0], near_kernel.shape[0]
    rows = n_tm * boxes
    grouped = signal.reshape(box_dev, peers, SUBLANES, samples)
    forward, inverse = spectral_tables(samples)
    operands = (
        grouped, source_boxes, near_boxes.T, trans_kernel, near_kernel, forward, inverse
    )
    hbm = pl.BlockSpec(memory_space=pltpu.HBM)
    field = pl.pallas_call(
        functools.partial(fused_kernel, n_tm, n_space),
        out_shape=pltpu.VMEM(grouped.shape, jnp.bfloat16),
        in_specs=[hbm] * len(operands),
        out_specs=pl.BlockSpec(memory_space=pl.ANY),
        scratch_shapes=[
            pltpu.VMEM((peers, box_dev, SUBLANES, LANES), jnp.bfloat16),
            pltpu.VMEM((n_tm + 2, boxes, SUBLANES, LANES), jnp.bfloat16),
            pltpu.VMEM((boxes, 2 * n_tm, SUBLANES, LANES), jnp.float32),
            pltpu.VMEM((n_tm, offsets, 3, SUBLANES, LANES), jnp.float32),
            pltpu.VMEM((slots, 3, SUBLANES, LANES), jnp.float32),
            pltpu.VMEM(trans_kernel.shape, jnp.float32),
            pltpu.VMEM((slots, LANES), jnp.float32),
            pltpu.VMEM(forward.shape, jnp.bfloat16),
            pltpu.VMEM(inverse.shape, jnp.bfloat16),
            pltpu.VMEM((n_tm, boxes, SUBLANES, LANES), jnp.bfloat16),
            pltpu.SMEM(source_boxes.shape, jnp.int32),
            pltpu.SMEM(near_boxes.shape[::-1], jnp.int32),
            pltpu.SemaphoreType.DMA,
            pltpu.SemaphoreType.DMA((n_tm + 2,)),
            pltpu.SemaphoreType.DMA,
            pltpu.SemaphoreType.DMA,
            pltpu.SemaphoreType.DMA((6,)),
            pltpu.SemaphoreType.DMA((box_dev,)),
            pltpu.SemaphoreType.REGULAR,
        ],
        compiler_params=pltpu.CompilerParams(
            collective_id=0, has_side_effects=True, vmem_limit_bytes=60*1024*1024
        ),
    )(*[pltpu.with_memory_space_constraint(x, pltpu.HBM) for x in operands])
    return field.reshape(signal.shape)


def routed(signal, source_boxes, near_boxes, trans_kernel, near_kernel):
    n_tm, n_space = lax.axis_size("tm"), lax.axis_size("space")
    box_dev, rays, samples = signal.shape
    rows = n_tm * n_space * box_dev
    fits = n_tm == 4 and n_space % SHARE == 0 and rays == n_tm * n_space * SUBLANES and samples == LANES and rows <= 2 * LANES
    chosen = fused_body if fits else body
    return chosen(signal, source_boxes, near_boxes, trans_kernel, near_kernel)


def solution(mesh):
    in_specs = (P("space", None, "tm"), P(), P(), P(None, "space", None), P())
    out_specs = P("space", None, "tm")
    return jax.shard_map(
        routed, mesh=mesh, in_specs=in_specs, out_specs=out_specs, check_vma=False
    )
```

```python
import functools

import jax
import jax.numpy as jnp
import numpy as np
from jax import lax
from jax.experimental import pallas as pl
from jax.experimental.pallas import tpu as pltpu
from jax.sharding import PartitionSpec as P

REACH = 2
MESH = pl.DeviceIdType.MESH
LANES = 128
SUBLANES = 8
SHARE = 4
ORDERS = ((0,3,1,2),(0,1,2,3),(0,1,2,3),(1,2,0,3))
def from_behind(shard, axis, by):
    size = lax.axis_size(axis)
    pairs = [(i, i + by) for i in range(size) if 0 <= i + by < size]
    return lax.ppermute(shard, axis, pairs)


def with_halo(block, sides, width):
    for axis, dim in sides:
        count = lax.axis_size(axis)
        forward = [(i, i + 1) for i in range(count - 1)]
        backward = [(target, source) for source, target in forward]
        low = lax.ppermute(
            lax.slice_in_dim(block, block.shape[dim] - width, None, axis=dim), axis, forward
        )
        high = lax.ppermute(lax.slice_in_dim(block, 0, width, axis=dim), axis, backward)
        block = jnp.concatenate([low, block, high], axis=dim)
    return block


def block_matrix(kernel):
    blocklen = kernel.shape[-1]
    leading = kernel.shape[:-1]
    zeroes = jnp.zeros(leading + (2 * blocklen,), jnp.bfloat16)
    widened = jnp.concatenate([zeroes, kernel.astype(jnp.bfloat16)], axis=-1)
    tiled = jnp.tile(widened, (1,) * len(leading) + (2 * blocklen,))
    trimmed = tiled[..., : 2 * blocklen * (3 * blocklen - 1)]
    skewed = trimmed.reshape(leading + (2 * blocklen, 3 * blocklen - 1))
    return skewed[..., :blocklen]


def body(signal, source_boxes, near_boxes, trans_kernel, near_kernel):
    box_dev = signal.shape[0]
    current_rays = lax.all_to_all(signal, "space", split_axis=1, concat_axis=0, tiled=True)
    earlier_rays = from_behind(current_rays, "tm", 1)
    pair_rays = jnp.concatenate([earlier_rays, current_rays], axis=-1)
    offsets = source_boxes.shape[1]
    far = jnp.zeros(current_rays.shape, jnp.float32)
    for offset in range(offsets):
        trans_mats = block_matrix(trans_kernel[offset])
        rows = jnp.take(pair_rays, source_boxes[:, offset], axis=0)
        far = far + jnp.einsum("brs,rst->brt", rows, trans_mats, preferred_element_type=jnp.float32)
    far_rays = far.astype(jnp.bfloat16)
    near_mats = block_matrix(near_kernel)
    slots = near_boxes.shape[1]
    earlier_box = from_behind(signal, "tm", 1)
    pair_box = jnp.concatenate([earlier_box, signal], axis=-1)
    padded = with_halo(pair_box, (("space", 0),), REACH)
    first = lax.axis_index("space") * box_dev
    own_near = lax.dynamic_slice_in_dim(near_boxes, first, box_dev, 0)
    local_rows = own_near - (first - REACH)
    near_sum = jnp.zeros(signal.shape, jnp.float32)
    for slot in range(slots):
        rows = jnp.take(padded, local_rows[:, slot], axis=0)
        near_sum = near_sum + jnp.einsum(
            "brs,st->brt", rows, near_mats[slot], preferred_element_type=jnp.float32
        )
    near_box = near_sum.astype(jnp.bfloat16)
    far_box = lax.all_to_all(far_rays, "space", split_axis=0, concat_axis=1, tiled=True)
    return (far_box.astype(jnp.float32) + near_box.astype(jnp.float32)).astype(jnp.bfloat16)


def spectral_tables(blocklen):
    lags = np.arange(2 * blocklen)[:, None]
    odd = 2 * np.arange(blocklen)[None, :] + 1
    angle = np.pi * lags * odd / (2 * blocklen)
    forward = np.concatenate([np.cos(angle), -np.sin(angle)], axis=1)
    later = angle[blocklen:].T
    inverse = np.concatenate([np.cos(later), -np.sin(later)], axis=0) / blocklen
    return jnp.asarray(forward, jnp.bfloat16), jnp.asarray(inverse, jnp.bfloat16)


def fused_kernel(
    n_tm,
    n_space,
    signal_ref,
    source_ref,
    near_ref,
    trans_ref,
    kernel_ref,
    forward_ref,
    inverse_ref,
    out_ref,
    staged,
    landed,
    spectra,
    responses,
    near_responses,
    trans_rows,
    near_rows,
    forward,
    inverse,
    leaving,
    sources,
    nears,
    in_send,
    in_recv,
    out_send,
    out_recv,
    local_sem,
    stage_sem,
    ready,
):
    tm, space = lax.axis_index("tm"), lax.axis_index("space")
    peers = n_tm * n_space
    last = n_tm - 1
    box_dev = signal_ref.shape[0]
    boxes = n_space * box_dev
    offsets = trans_ref.shape[0]
    slots = kernel_ref.shape[0]
    on_first, on_last = tm == 0, tm == last
    on_edge = jnp.logical_or(on_first, on_last)
    on_middle = jnp.logical_not(on_edge)

    orders = ORDERS
    def awaited(line, turn):
        def needs(item):
            if line in (0, last) and item == last:
                return {0, last + 2} if line else {last + 1}
            shift = 1 if line == last else 0
            return {item + shift, item + 1 + shift} - ({0} if line < last else set())

        before = [needs(item) for item in orders[line][:turn]]
        return sorted(needs(orders[line][turn]).difference(*before))

    def item_at(turn):
        item = orders[0][turn]
        for line in range(1, n_tm):
            item = jnp.where(tm == line, orders[line][turn], item)
        return item

    def swapped(item):
        return jnp.logical_and(on_edge, item == last)

    def group_of(item):
        return jnp.where(swapped(item), last - tm, tm)

    def places(item):
        shift = jnp.where(on_last, 1, 0)
        return jnp.where(swapped(item), 0, item + shift), item + 1 + shift

    def skipping(position, mine):
        return position + jnp.where(position >= mine, 1, 0)

    own_boxes = pl.ds(space * box_dev, box_dev)
    barrier = pltpu.get_barrier_semaphore()

    def greet(to_tm):
        for to_space in range(n_space):
            to = (to_tm, to_space)
            pl.semaphore_signal(barrier, inc=1, device_id=to, device_id_type=MESH)

    @pl.when(tm < last)
    def _():
        greet(0)

    for to_tm in range(1, n_tm):
        greet(to_tm)

    fetches = [
        pltpu.make_async_copy(trans_ref, trans_rows, local_sem.at[0]),
        pltpu.make_async_copy(kernel_ref, near_rows, local_sem.at[1]),
        pltpu.make_async_copy(source_ref, sources, local_sem.at[2]),
        pltpu.make_async_copy(near_ref, nears, local_sem.at[3]),
        pltpu.make_async_copy(forward_ref, forward, local_sem.at[4]),
        pltpu.make_async_copy(inverse_ref, inverse, local_sem.at[5]),
    ]
    stagings = [
        pltpu.make_async_copy(signal_ref.at[nth], staged.at[:, nth], stage_sem.at[nth])
        for nth in range(box_dev)
    ]
    for fetch in stagings + fetches:
        fetch.start()
    for staging in stagings:
        staging.wait()

    def place_of(place):
        return landed.at[place, own_boxes]

    def send_in(to_tm, to_space, group, place):
        pltpu.make_async_remote_copy(
            src_ref=staged.at[to_space * n_tm + group],
            dst_ref=place_of(place),
            send_sem=in_send,
            recv_sem=in_recv.at[place],
            device_id=(to_tm, to_space),
            device_id_type=MESH,
        ).start()

    def keep_in(group, place):
        source = staged.at[space * n_tm + group]
        pltpu.make_async_copy(source, place_of(place), in_recv.at[place]).start()

    @pl.when(on_first)
    def _():
        pl.semaphore_wait(barrier, last * n_space)
        for position in reversed(range(last * n_space - 1)):
            peer = skipping(position, space * last)
            to_tm, to_space = peer % last, peer // last
            send_in(to_tm, to_space, to_tm, 1)
        for position in reversed(range(n_space - 1)):
            send_in(0, skipping(position, space), last, n_tm)
        keep_in(0, 1)
        keep_in(last, n_tm)
        pl.semaphore_wait(ready, n_space)
        for to_space in reversed(range(n_space)):
            send_in(last, to_space, last, 1)

    @pl.when(on_middle)
    def _():
        pl.semaphore_wait(barrier, peers)
        for position in reversed(range(peers - 1)):
            peer = skipping(position, space * n_tm + tm)
            to_tm, to_space = peer % n_tm, peer // n_tm
            send_in(to_tm, to_space, to_tm, tm + 1)
        keep_in(tm, tm + 1)

        @pl.when(tm == last - 1)
        def _():
            for to_space in reversed(range(n_space)):
                send_in(last, to_space, 0, 0)

    @pl.when(on_last)
    def _():
        pl.semaphore_wait(barrier, peers)
        for to_space in range(n_space):
            pl.semaphore_signal(ready, inc=1, device_id=(0, to_space), device_id_type=MESH)
        for position in reversed(range(last * n_space - 1)):
            peer = skipping(position, space * last + last - 1)
            to_tm, to_space = peer % last + 1, peer // last
            send_in(to_tm, to_space, to_tm, n_tm)
        for position in reversed(range(n_space - 1)):
            send_in(last, skipping(position, space), 0, n_tm + 1)
        keep_in(last, n_tm)
        keep_in(0, n_tm + 1)

    for fetch in fetches:
        fetch.wait()

    def respond(lags):
        return jnp.dot(
            lags.astype(jnp.bfloat16), forward[0:LANES, :], preferred_element_type=jnp.float32
        )

    def keep_response(where, both):
        real, imag = both[:, :LANES], both[:, LANES:]
        where[0] = real
        where[1] = imag - real
        where[2] = imag + real

    for turn in range(n_tm):
        first_ray = pl.multiple_of(group_of(item_at(turn)) * SUBLANES, SUBLANES)
        far = respond(
            trans_rows[:, pl.ds(first_ray, SUBLANES), :].reshape(offsets * SUBLANES, LANES)
        )
        for entry in range(offsets):
            these = slice(entry * SUBLANES, (entry + 1) * SUBLANES)
            keep_response(responses.at[turn, entry], far[these])
    near = respond(near_rows[...])
    for slot in range(slots):
        both = jnp.broadcast_to(near[slot : slot + 1, :], (SUBLANES, 2 * LANES))
        keep_response(near_responses.at[slot], both)

    def arrive(place):
        arrived = landed.at[place]
        pltpu.make_async_copy(arrived, arrived, in_recv.at[place]).wait()

    def unpacked(place):
        flat = landed[place].astype(jnp.float32).reshape(boxes * SUBLANES, LANES)
        return flat.astype(jnp.bfloat16)

    def transform(turn):
        earlier, current = places(item_at(turn))
        pair = jnp.concatenate([unpacked(earlier), unpacked(current)], axis=1)
        both = jnp.dot(pair, forward[...], preferred_element_type=jnp.float32)
        spectra[:, 2 * turn] = both[:, :LANES].reshape(boxes, SUBLANES, LANES)
        spectra[:, 2 * turn + 1] = both[:, LANES:].reshape(boxes, SUBLANES, LANES)

    def finish(turn, first):
        targets = [first * box_dev + nth for nth in range(SHARE * box_dev)]
        sums = [None] * len(targets)
        for entry in range(offsets + slots):
            if entry < offsets:
                factors = [responses[turn, entry, part] for part in range(3)]
            else:
                factors = [near_responses[entry - offsets, part] for part in range(3)]
            for place, box in enumerate(targets):
                origin = sources[box, entry] if entry < offsets else nears[entry - offsets, box]
                a, b = (spectra[origin, 2 * turn + part] for part in range(2))
                terms = [factors[0] * (a + b), factors[1] * a, factors[2] * b]
                if entry:
                    terms = [x + y for x, y in zip(sums[place], terms)]
                sums[place] = terms
        real = jnp.concatenate([x - z for x, y, z in sums], axis=0)
        imag = jnp.concatenate([x + y for x, y, z in sums], axis=0)
        spectrum = jnp.concatenate([real, imag], axis=1).astype(jnp.bfloat16)
        field = jnp.dot(spectrum, inverse[...], preferred_element_type=jnp.float32)
        for nth, box in enumerate(targets):
            leaving[turn, box] = field[nth * SUBLANES : (nth + 1) * SUBLANES].astype(jnp.bfloat16)

    def deliver(turn, first):
        item = item_at(turn)
        to_tm = jnp.where(swapped(item), tm, item + jnp.where(on_last, 1, 0))
        target = out_ref.at[:, space * n_tm + group_of(item)]
        own_line = to_tm == tm
        own_here = jnp.logical_and(own_line, space // SHARE == first // SHARE)

        def source(to_space):
            return leaving.at[turn, pl.ds(to_space * box_dev, box_dev)]

        def send_out(to_space):
            pltpu.make_async_remote_copy(
                src_ref=source(to_space),
                dst_ref=target,
                send_sem=out_send,
                recv_sem=out_recv,
                device_id=(to_tm, to_space),
                device_id_type=MESH,
            ).start()

        @pl.when(jnp.logical_not(own_here))
        def _():
            for nth in range(SHARE):
                send_out(first + nth)

        @pl.when(own_here)
        def _():
            for position in range(SHARE - 1):
                send_out(first + skipping(position, space - first))
            pltpu.make_async_copy(source(space), target, out_recv).start()

    @pl.when(tm < last)
    def _():
        landed[0] = jnp.zeros(landed.shape[1:], jnp.bfloat16)

    for turn in range(n_tm):
        for line in range(n_tm):
            if awaited(line, turn):

                @pl.when(tm == line)
                def _():
                    for place in awaited(line, turn):
                        arrive(place)

        transform(turn)

        for first in range(0, n_space, SHARE):
            finish(turn, first)
            deliver(turn, first)

    def settle(pieces, sem):
        sent = staged.at[pl.ds(0, pieces)]
        pltpu.make_async_copy(sent, sent, sem).wait()

    @pl.when(on_first)
    def _():
        settle(last * n_space - 1 + n_space - 1, in_send)
        settle(n_space, in_send)

    @pl.when(on_middle)
    def _():
        settle(peers - 1, in_send)

        @pl.when(tm == last - 1)
        def _():
            settle(n_space, in_send)

    @pl.when(on_last)
    def _():
        settle(last * n_space - 1 + n_space - 1, in_send)

    pltpu.make_async_copy(out_ref, out_ref, out_recv).wait()

    @pl.when(on_middle)
    def _():
        settle(peers - 1, out_send)

    @pl.when(on_edge)
    def _():
        settle(peers - 2, out_send)


def fused_body(signal, source_boxes, near_boxes, trans_kernel, near_kernel):
    n_tm, n_space = lax.axis_size("tm"), lax.axis_size("space")
    peers = n_tm * n_space
    box_dev, rays, samples = signal.shape
    boxes = box_dev * n_space
    offsets, slots = trans_kernel.shape[0], near_kernel.shape[0]
    rows = n_tm * boxes
    grouped = signal.reshape(box_dev, peers, SUBLANES, samples)
    forward, inverse = spectral_tables(samples)
    operands = (
        grouped, source_boxes, near_boxes.T, trans_kernel, near_kernel, forward, inverse
    )
    hbm = pl.BlockSpec(memory_space=pltpu.HBM)
    field = pl.pallas_call(
        functools.partial(fused_kernel, n_tm, n_space),
        out_shape=pltpu.VMEM(grouped.shape, jnp.bfloat16),
        in_specs=[hbm] * len(operands),
        out_specs=pl.BlockSpec(memory_space=pl.ANY),
        scratch_shapes=[
            pltpu.VMEM((peers, box_dev, SUBLANES, LANES), jnp.bfloat16),
            pltpu.VMEM((n_tm + 2, boxes, SUBLANES, LANES), jnp.bfloat16),
            pltpu.VMEM((boxes, 2 * n_tm, SUBLANES, LANES), jnp.float32),
            pltpu.VMEM((n_tm, offsets, 3, SUBLANES, LANES), jnp.float32),
            pltpu.VMEM((slots, 3, SUBLANES, LANES), jnp.float32),
            pltpu.VMEM(trans_kernel.shape, jnp.float32),
            pltpu.VMEM((slots, LANES), jnp.float32),
            pltpu.VMEM(forward.shape, jnp.bfloat16),
            pltpu.VMEM(inverse.shape, jnp.bfloat16),
            pltpu.VMEM((n_tm, boxes, SUBLANES, LANES), jnp.bfloat16),
            pltpu.SMEM(source_boxes.shape, jnp.int32),
            pltpu.SMEM(near_boxes.shape[::-1], jnp.int32),
            pltpu.SemaphoreType.DMA,
            pltpu.SemaphoreType.DMA((n_tm + 2,)),
            pltpu.SemaphoreType.DMA,
            pltpu.SemaphoreType.DMA,
            pltpu.SemaphoreType.DMA((6,)),
            pltpu.SemaphoreType.DMA((box_dev,)),
            pltpu.SemaphoreType.REGULAR,
        ],
        compiler_params=pltpu.CompilerParams(
            collective_id=0, has_side_effects=True, vmem_limit_bytes=60*1024*1024
        ),
    )(*[pltpu.with_memory_space_constraint(x, pltpu.HBM) for x in operands])
    return field.reshape(signal.shape)


def routed(signal, source_boxes, near_boxes, trans_kernel, near_kernel):
    n_tm, n_space = lax.axis_size("tm"), lax.axis_size("space")
    box_dev, rays, samples = signal.shape
    rows = n_tm * n_space * box_dev
    fits = n_tm == 4 and n_space % SHARE == 0 and rays == n_tm * n_space * SUBLANES and samples == LANES and rows <= 2 * LANES
    chosen = fused_body if fits else body
    return chosen(signal, source_boxes, near_boxes, trans_kernel, near_kernel)


def solution(mesh):
    in_specs = (P("space", None, "tm"), P(), P(), P(None, "space", None), P())
    out_specs = P("space", None, "tm")
    return jax.shard_map(
        routed, mesh=mesh, in_specs=in_specs, out_specs=out_specs, check_vma=False
    )
```

```python
import functools

import jax
import jax.numpy as jnp
import numpy as np
from jax import lax
from jax.experimental import pallas as pl
from jax.experimental.pallas import tpu as pltpu
from jax.sharding import PartitionSpec as P

REACH = 2
MESH = pl.DeviceIdType.MESH
LANES = 128
SUBLANES = 8
SHARE = 4
ORDERS = ((0,3,1,2),(0,1,2,3),(0,1,2,3),(1,2,0,3))
def from_behind(shard, axis, by):
    size = lax.axis_size(axis)
    pairs = [(i, i + by) for i in range(size) if 0 <= i + by < size]
    return lax.ppermute(shard, axis, pairs)


def with_halo(block, sides, width):
    for axis, dim in sides:
        count = lax.axis_size(axis)
        forward = [(i, i + 1) for i in range(count - 1)]
        backward = [(target, source) for source, target in forward]
        low = lax.ppermute(
            lax.slice_in_dim(block, block.shape[dim] - width, None, axis=dim), axis, forward
        )
        high = lax.ppermute(lax.slice_in_dim(block, 0, width, axis=dim), axis, backward)
        block = jnp.concatenate([low, block, high], axis=dim)
    return block


def block_matrix(kernel):
    blocklen = kernel.shape[-1]
    leading = kernel.shape[:-1]
    zeroes = jnp.zeros(leading + (2 * blocklen,), jnp.bfloat16)
    widened = jnp.concatenate([zeroes, kernel.astype(jnp.bfloat16)], axis=-1)
    tiled = jnp.tile(widened, (1,) * len(leading) + (2 * blocklen,))
    trimmed = tiled[..., : 2 * blocklen * (3 * blocklen - 1)]
    skewed = trimmed.reshape(leading + (2 * blocklen, 3 * blocklen - 1))
    return skewed[..., :blocklen]


def body(signal, source_boxes, near_boxes, trans_kernel, near_kernel):
    box_dev = signal.shape[0]
    current_rays = lax.all_to_all(signal, "space", split_axis=1, concat_axis=0, tiled=True)
    earlier_rays = from_behind(current_rays, "tm", 1)
    pair_rays = jnp.concatenate([earlier_rays, current_rays], axis=-1)
    offsets = source_boxes.shape[1]
    far = jnp.zeros(current_rays.shape, jnp.float32)
    for offset in range(offsets):
        trans_mats = block_matrix(trans_kernel[offset])
        rows = jnp.take(pair_rays, source_boxes[:, offset], axis=0)
        far = far + jnp.einsum("brs,rst->brt", rows, trans_mats, preferred_element_type=jnp.float32)
    far_rays = far.astype(jnp.bfloat16)
    near_mats = block_matrix(near_kernel)
    slots = near_boxes.shape[1]
    earlier_box = from_behind(signal, "tm", 1)
    pair_box = jnp.concatenate([earlier_box, signal], axis=-1)
    padded = with_halo(pair_box, (("space", 0),), REACH)
    first = lax.axis_index("space") * box_dev
    own_near = lax.dynamic_slice_in_dim(near_boxes, first, box_dev, 0)
    local_rows = own_near - (first - REACH)
    near_sum = jnp.zeros(signal.shape, jnp.float32)
    for slot in range(slots):
        rows = jnp.take(padded, local_rows[:, slot], axis=0)
        near_sum = near_sum + jnp.einsum(
            "brs,st->brt", rows, near_mats[slot], preferred_element_type=jnp.float32
        )
    near_box = near_sum.astype(jnp.bfloat16)
    far_box = lax.all_to_all(far_rays, "space", split_axis=0, concat_axis=1, tiled=True)
    return (far_box.astype(jnp.float32) + near_box.astype(jnp.float32)).astype(jnp.bfloat16)


def spectral_tables(blocklen):
    lags = np.arange(2 * blocklen)[:, None]
    odd = 2 * np.arange(blocklen)[None, :] + 1
    angle = np.pi * lags * odd / (2 * blocklen)
    forward = np.concatenate([np.cos(angle), -np.sin(angle)], axis=1)
    later = angle[blocklen:].T
    inverse = np.concatenate([np.cos(later), -np.sin(later)], axis=0) / blocklen
    return jnp.asarray(forward, jnp.bfloat16), jnp.asarray(inverse, jnp.bfloat16)


def fused_kernel(
    n_tm,
    n_space,
    signal_ref,
    source_ref,
    near_ref,
    trans_ref,
    kernel_ref,
    forward_ref,
    inverse_ref,
    out_ref,
    staged,
    landed,
    spectra,
    responses,
    near_responses,
    trans_rows,
    near_rows,
    forward,
    inverse,
    leaving,
    sources,
    nears,
    in_send,
    in_recv,
    out_send,
    out_recv,
    local_sem,
    stage_sem,
    ready,
):
    tm, space = lax.axis_index("tm"), lax.axis_index("space")
    peers = n_tm * n_space
    last = n_tm - 1
    box_dev = signal_ref.shape[0]
    boxes = n_space * box_dev
    offsets = trans_ref.shape[0]
    slots = kernel_ref.shape[0]
    on_first, on_last = tm == 0, tm == last
    on_edge = jnp.logical_or(on_first, on_last)
    on_middle = jnp.logical_not(on_edge)

    orders = ORDERS
    def awaited(line, turn):
        def needs(item):
            if line in (0, last) and item == last:
                return {0, last + 2} if line else {last + 1}
            shift = 1 if line == last else 0
            return {item + shift, item + 1 + shift} - ({0} if line < last else set())

        before = [needs(item) for item in orders[line][:turn]]
        return sorted(needs(orders[line][turn]).difference(*before))

    def item_at(turn):
        item = orders[0][turn]
        for line in range(1, n_tm):
            item = jnp.where(tm == line, orders[line][turn], item)
        return item

    def swapped(item):
        return jnp.logical_and(on_edge, item == last)

    def group_of(item):
        return jnp.where(swapped(item), last - tm, tm)

    def places(item):
        shift = jnp.where(on_last, 1, 0)
        return jnp.where(swapped(item), 0, item + shift), item + 1 + shift

    def skipping(position, mine):
        return position + jnp.where(position >= mine, 1, 0)

    own_boxes = pl.ds(space * box_dev, box_dev)
    barrier = pltpu.get_barrier_semaphore()

    def greet(to_tm):
        for to_space in range(n_space):
            to = (to_tm, to_space)
            pl.semaphore_signal(barrier, inc=1, device_id=to, device_id_type=MESH)

    @pl.when(tm < last)
    def _():
        greet(0)

    for to_tm in range(1, n_tm):
        greet(to_tm)

    fetches = [
        pltpu.make_async_copy(trans_ref, trans_rows, local_sem.at[0]),
        pltpu.make_async_copy(kernel_ref, near_rows, local_sem.at[1]),
        pltpu.make_async_copy(source_ref, sources, local_sem.at[2]),
        pltpu.make_async_copy(near_ref, nears, local_sem.at[3]),
        pltpu.make_async_copy(forward_ref, forward, local_sem.at[4]),
        pltpu.make_async_copy(inverse_ref, inverse, local_sem.at[5]),
    ]
    stagings = [
        pltpu.make_async_copy(signal_ref.at[nth], staged.at[:, nth], stage_sem.at[nth])
        for nth in range(box_dev)
    ]
    for fetch in stagings + fetches:
        fetch.start()
    for staging in stagings:
        staging.wait()

    def place_of(place):
        return landed.at[place, own_boxes]

    def send_in(to_tm, to_space, group, place):
        pltpu.make_async_remote_copy(
            src_ref=staged.at[to_space * n_tm + group],
            dst_ref=place_of(place),
            send_sem=in_send,
            recv_sem=in_recv.at[place],
            device_id=(to_tm, to_space),
            device_id_type=MESH,
        ).start()

    def keep_in(group, place):
        source = staged.at[space * n_tm + group]
        pltpu.make_async_copy(source, place_of(place), in_recv.at[place]).start()

    @pl.when(on_first)
    def _():
        pl.semaphore_wait(barrier, last * n_space)
        for position in reversed(range(last * n_space - 1)):
            far = last * n_space - 2 - position
            peer = skipping(jnp.where(space < n_space // 2, position, far), space * last)
            to_tm, to_space = peer % last, peer // last
            send_in(to_tm, to_space, to_tm, 1)
        for position in reversed(range(n_space - 1)):
            send_in(0, skipping(position, space), last, n_tm)
        keep_in(0, 1)
        keep_in(last, n_tm)
        pl.semaphore_wait(ready, n_space)
        for to_space in reversed(range(n_space)):
            send_in(last, to_space, last, 1)

    @pl.when(on_middle)
    def _():
        pl.semaphore_wait(barrier, peers)
        for position in reversed(range(peers - 1)):
            place = jnp.where(space < n_space // 2, position, peers - 2 - position)
            peer = skipping(place, space * n_tm + tm)
            to_tm, to_space = peer % n_tm, peer // n_tm
            send_in(to_tm, to_space, to_tm, tm + 1)
        keep_in(tm, tm + 1)

        @pl.when(tm == last - 1)
        def _():
            for to_space in reversed(range(n_space)):
                send_in(last, to_space, 0, 0)

    @pl.when(on_last)
    def _():
        pl.semaphore_wait(barrier, peers)
        for to_space in range(n_space):
            pl.semaphore_signal(ready, inc=1, device_id=(0, to_space), device_id_type=MESH)
        for position in reversed(range(last * n_space - 1)):
            far = last * n_space - 2 - position
            peer = skipping(jnp.where(space < n_space // 2, position, far), space * last + last - 1)
            to_tm, to_space = peer % last + 1, peer // last
            send_in(to_tm, to_space, to_tm, n_tm)
        for position in reversed(range(n_space - 1)):
            send_in(last, skipping(position, space), 0, n_tm + 1)
        keep_in(last, n_tm)
        keep_in(0, n_tm + 1)

    for fetch in fetches:
        fetch.wait()

    def respond(lags):
        return jnp.dot(
            lags.astype(jnp.bfloat16), forward[0:LANES, :], preferred_element_type=jnp.float32
        )

    def keep_response(where, both):
        real, imag = both[:, :LANES], both[:, LANES:]
        where[0] = real
        where[1] = imag - real
        where[2] = imag + real

    for turn in range(n_tm):
        first_ray = pl.multiple_of(group_of(item_at(turn)) * SUBLANES, SUBLANES)
        far = respond(
            trans_rows[:, pl.ds(first_ray, SUBLANES), :].reshape(offsets * SUBLANES, LANES)
        )
        for entry in range(offsets):
            these = slice(entry * SUBLANES, (entry + 1) * SUBLANES)
            keep_response(responses.at[turn, entry], far[these])
    near = respond(near_rows[...])
    for slot in range(slots):
        both = jnp.broadcast_to(near[slot : slot + 1, :], (SUBLANES, 2 * LANES))
        keep_response(near_responses.at[slot], both)

    def arrive(place):
        arrived = landed.at[place]
        pltpu.make_async_copy(arrived, arrived, in_recv.at[place]).wait()

    def unpacked(place):
        flat = landed[place].astype(jnp.float32).reshape(boxes * SUBLANES, LANES)
        return flat.astype(jnp.bfloat16)

    def transform(turn):
        earlier, current = places(item_at(turn))
        pair = jnp.concatenate([unpacked(earlier), unpacked(current)], axis=1)
        both = jnp.dot(pair, forward[...], preferred_element_type=jnp.float32)
        spectra[:, 2 * turn] = both[:, :LANES].reshape(boxes, SUBLANES, LANES)
        spectra[:, 2 * turn + 1] = both[:, LANES:].reshape(boxes, SUBLANES, LANES)

    def finish(turn, first, end):
        targets = list(range(first * box_dev, end * box_dev))
        sums = [None] * len(targets)
        for entry in range(offsets + slots):
            if entry < offsets:
                factors = [responses[turn, entry, part] for part in range(3)]
            else:
                factors = [near_responses[entry - offsets, part] for part in range(3)]
            for place, box in enumerate(targets):
                origin = sources[box, entry] if entry < offsets else nears[entry - offsets, box]
                a, b = (spectra[origin, 2 * turn + part] for part in range(2))
                terms = [factors[0] * (a + b), factors[1] * a, factors[2] * b]
                if entry:
                    terms = [x + y for x, y in zip(sums[place], terms)]
                sums[place] = terms
        real = jnp.concatenate([x - z for x, y, z in sums], axis=0)
        imag = jnp.concatenate([x + y for x, y, z in sums], axis=0)
        spectrum = jnp.concatenate([real, imag], axis=1).astype(jnp.bfloat16)
        field = jnp.dot(spectrum, inverse[...], preferred_element_type=jnp.float32)
        for nth, box in enumerate(targets):
            leaving[turn, box] = field[nth * SUBLANES : (nth + 1) * SUBLANES].astype(jnp.bfloat16)

    def deliver(turn, first, end):
        item = item_at(turn)
        to_tm = jnp.where(swapped(item), tm, item + jnp.where(on_last, 1, 0))
        target = out_ref.at[:, space * n_tm + group_of(item)]
        own_line = to_tm == tm
        here = jnp.logical_and(space >= first, space < end)
        own_here = jnp.logical_and(own_line, here)

        def source(to_space):
            return leaving.at[turn, pl.ds(to_space * box_dev, box_dev)]

        def send_out(to_space):
            pltpu.make_async_remote_copy(
                src_ref=source(to_space),
                dst_ref=target,
                send_sem=out_send,
                recv_sem=out_recv,
                device_id=(to_tm, to_space),
                device_id_type=MESH,
            ).start()

        @pl.when(jnp.logical_not(own_here))
        def _():
            for to_space in range(first, end):
                send_out(to_space)

        @pl.when(own_here)
        def _():
            for position in range(first, end - 1):
                send_out(skipping(position, space))
            pltpu.make_async_copy(source(space), target, out_recv).start()

    @pl.when(tm < last)
    def _():
        landed[0] = jnp.zeros(landed.shape[1:], jnp.bfloat16)

    def take(turn):
        for line in range(n_tm):
            if awaited(line, turn):

                @pl.when(tm == line)
                def _():
                    for place in awaited(line, turn):
                        arrive(place)

        transform(turn)

    def serve(turn, *shares):
        for first, end in shares:
            finish(turn, first, end)
            deliver(turn, first, end)

    near, rest = [(0, 4)], [(4, n_space)]
    for turn in range(2):
        take(turn)
        serve(turn, *near, *rest)
    for turn in range(2, n_tm):
        take(turn)
        serve(turn, *near)
    for turn in range(2, n_tm):
        serve(turn, *rest)

    def settle(pieces, sem):
        sent = staged.at[pl.ds(0, pieces)]
        pltpu.make_async_copy(sent, sent, sem).wait()

    @pl.when(on_first)
    def _():
        settle(last * n_space - 1 + n_space - 1, in_send)
        settle(n_space, in_send)

    @pl.when(on_middle)
    def _():
        settle(peers - 1, in_send)

        @pl.when(tm == last - 1)
        def _():
            settle(n_space, in_send)

    @pl.when(on_last)
    def _():
        settle(last * n_space - 1 + n_space - 1, in_send)

    pltpu.make_async_copy(out_ref, out_ref, out_recv).wait()

    @pl.when(on_middle)
    def _():
        settle(peers - 1, out_send)

    @pl.when(on_edge)
    def _():
        settle(peers - 2, out_send)


def fused_body(signal, source_boxes, near_boxes, trans_kernel, near_kernel):
    n_tm, n_space = lax.axis_size("tm"), lax.axis_size("space")
    peers = n_tm * n_space
    box_dev, rays, samples = signal.shape
    boxes = box_dev * n_space
    offsets, slots = trans_kernel.shape[0], near_kernel.shape[0]
    rows = n_tm * boxes
    grouped = signal.reshape(box_dev, peers, SUBLANES, samples)
    forward, inverse = spectral_tables(samples)
    operands = (
        grouped, source_boxes, near_boxes.T, trans_kernel, near_kernel, forward, inverse
    )
    hbm = pl.BlockSpec(memory_space=pltpu.HBM)
    field = pl.pallas_call(
        functools.partial(fused_kernel, n_tm, n_space),
        out_shape=pltpu.VMEM(grouped.shape, jnp.bfloat16),
        in_specs=[hbm] * len(operands),
        out_specs=pl.BlockSpec(memory_space=pl.ANY),
        scratch_shapes=[
            pltpu.VMEM((peers, box_dev, SUBLANES, LANES), jnp.bfloat16),
            pltpu.VMEM((n_tm + 2, boxes, SUBLANES, LANES), jnp.bfloat16),
            pltpu.VMEM((boxes, 2 * n_tm, SUBLANES, LANES), jnp.float32),
            pltpu.VMEM((n_tm, offsets, 3, SUBLANES, LANES), jnp.float32),
            pltpu.VMEM((slots, 3, SUBLANES, LANES), jnp.float32),
            pltpu.VMEM(trans_kernel.shape, jnp.float32),
            pltpu.VMEM((slots, LANES), jnp.float32),
            pltpu.VMEM(forward.shape, jnp.bfloat16),
            pltpu.VMEM(inverse.shape, jnp.bfloat16),
            pltpu.VMEM((n_tm, boxes, SUBLANES, LANES), jnp.bfloat16),
            pltpu.SMEM(source_boxes.shape, jnp.int32),
            pltpu.SMEM(near_boxes.shape[::-1], jnp.int32),
            pltpu.SemaphoreType.DMA,
            pltpu.SemaphoreType.DMA((n_tm + 2,)),
            pltpu.SemaphoreType.DMA,
            pltpu.SemaphoreType.DMA,
            pltpu.SemaphoreType.DMA((6,)),
            pltpu.SemaphoreType.DMA((box_dev,)),
            pltpu.SemaphoreType.REGULAR,
        ],
        compiler_params=pltpu.CompilerParams(
            collective_id=0, has_side_effects=True, vmem_limit_bytes=60*1024*1024
        ),
    )(*[pltpu.with_memory_space_constraint(x, pltpu.HBM) for x in operands])
    return field.reshape(signal.shape)


def routed(signal, source_boxes, near_boxes, trans_kernel, near_kernel):
    n_tm, n_space = lax.axis_size("tm"), lax.axis_size("space")
    box_dev, rays, samples = signal.shape
    rows = n_tm * n_space * box_dev
    fits = n_tm == 4 and n_space % SHARE == 0 and rays == n_tm * n_space * SUBLANES and samples == LANES and rows <= 2 * LANES
    chosen = fused_body if fits else body
    return chosen(signal, source_boxes, near_boxes, trans_kernel, near_kernel)


def solution(mesh):
    in_specs = (P("space", None, "tm"), P(), P(), P(None, "space", None), P())
    out_specs = P("space", None, "tm")
    return jax.shard_map(
        routed, mesh=mesh, in_specs=in_specs, out_specs=out_specs, check_vma=False
    )
```

```python
import functools

import jax
import jax.numpy as jnp
import numpy as np
from jax import lax
from jax.experimental import pallas as pl
from jax.experimental.pallas import tpu as pltpu
from jax.sharding import PartitionSpec as P

REACH = 2
MESH = pl.DeviceIdType.MESH
LANES = 128
SUBLANES = 8
SHARE = 8
ORDERS = ((0,3,1,2),(0,1,2,3),(0,1,2,3),(1,2,0,3))
def from_behind(shard, axis, by):
    size = lax.axis_size(axis)
    pairs = [(i, i + by) for i in range(size) if 0 <= i + by < size]
    return lax.ppermute(shard, axis, pairs)


def with_halo(block, sides, width):
    for axis, dim in sides:
        count = lax.axis_size(axis)
        forward = [(i, i + 1) for i in range(count - 1)]
        backward = [(target, source) for source, target in forward]
        low = lax.ppermute(
            lax.slice_in_dim(block, block.shape[dim] - width, None, axis=dim), axis, forward
        )
        high = lax.ppermute(lax.slice_in_dim(block, 0, width, axis=dim), axis, backward)
        block = jnp.concatenate([low, block, high], axis=dim)
    return block


def block_matrix(kernel):
    blocklen = kernel.shape[-1]
    leading = kernel.shape[:-1]
    zeroes = jnp.zeros(leading + (2 * blocklen,), jnp.bfloat16)
    widened = jnp.concatenate([zeroes, kernel.astype(jnp.bfloat16)], axis=-1)
    tiled = jnp.tile(widened, (1,) * len(leading) + (2 * blocklen,))
    trimmed = tiled[..., : 2 * blocklen * (3 * blocklen - 1)]
    skewed = trimmed.reshape(leading + (2 * blocklen, 3 * blocklen - 1))
    return skewed[..., :blocklen]


def body(signal, source_boxes, near_boxes, trans_kernel, near_kernel):
    box_dev = signal.shape[0]
    current_rays = lax.all_to_all(signal, "space", split_axis=1, concat_axis=0, tiled=True)
    earlier_rays = from_behind(current_rays, "tm", 1)
    pair_rays = jnp.concatenate([earlier_rays, current_rays], axis=-1)
    offsets = source_boxes.shape[1]
    far = jnp.zeros(current_rays.shape, jnp.float32)
    for offset in range(offsets):
        trans_mats = block_matrix(trans_kernel[offset])
        rows = jnp.take(pair_rays, source_boxes[:, offset], axis=0)
        far = far + jnp.einsum("brs,rst->brt", rows, trans_mats, preferred_element_type=jnp.float32)
    far_rays = far.astype(jnp.bfloat16)
    near_mats = block_matrix(near_kernel)
    slots = near_boxes.shape[1]
    earlier_box = from_behind(signal, "tm", 1)
    pair_box = jnp.concatenate([earlier_box, signal], axis=-1)
    padded = with_halo(pair_box, (("space", 0),), REACH)
    first = lax.axis_index("space") * box_dev
    own_near = lax.dynamic_slice_in_dim(near_boxes, first, box_dev, 0)
    local_rows = own_near - (first - REACH)
    near_sum = jnp.zeros(signal.shape, jnp.float32)
    for slot in range(slots):
        rows = jnp.take(padded, local_rows[:, slot], axis=0)
        near_sum = near_sum + jnp.einsum(
            "brs,st->brt", rows, near_mats[slot], preferred_element_type=jnp.float32
        )
    near_box = near_sum.astype(jnp.bfloat16)
    far_box = lax.all_to_all(far_rays, "space", split_axis=0, concat_axis=1, tiled=True)
    return (far_box.astype(jnp.float32) + near_box.astype(jnp.float32)).astype(jnp.bfloat16)


def spectral_tables(blocklen):
    lags = np.arange(2 * blocklen)[:, None]
    odd = 2 * np.arange(blocklen)[None, :] + 1
    angle = np.pi * lags * odd / (2 * blocklen)
    forward = np.concatenate([np.cos(angle), -np.sin(angle)], axis=1)
    later = angle[blocklen:].T
    inverse = np.concatenate([np.cos(later), -np.sin(later)], axis=0) / blocklen
    return jnp.asarray(forward, jnp.bfloat16), jnp.asarray(inverse, jnp.bfloat16)


def fused_kernel(
    n_tm,
    n_space,
    signal_ref,
    source_ref,
    near_ref,
    trans_ref,
    kernel_ref,
    forward_ref,
    inverse_ref,
    out_ref,
    staged,
    landed,
    spectra,
    responses,
    near_responses,
    trans_rows,
    near_rows,
    forward,
    inverse,
    leaving,
    sources,
    nears,
    in_send,
    in_recv,
    out_send,
    out_recv,
    local_sem,
    stage_sem,
    ready,
):
    tm, space = lax.axis_index("tm"), lax.axis_index("space")
    peers = n_tm * n_space
    last = n_tm - 1
    box_dev = signal_ref.shape[0]
    boxes = n_space * box_dev
    offsets = trans_ref.shape[0]
    slots = kernel_ref.shape[0]
    on_first, on_last = tm == 0, tm == last
    on_edge = jnp.logical_or(on_first, on_last)
    on_middle = jnp.logical_not(on_edge)

    orders = ORDERS
    def awaited(line, turn):
        def needs(item):
            if line in (0, last) and item == last:
                return {0, last + 2} if line else {last + 1}
            shift = 1 if line == last else 0
            return {item + shift, item + 1 + shift} - ({0} if line < last else set())

        before = [needs(item) for item in orders[line][:turn]]
        return sorted(needs(orders[line][turn]).difference(*before))

    def item_at(turn):
        item = orders[0][turn]
        for line in range(1, n_tm):
            item = jnp.where(tm == line, orders[line][turn], item)
        return item

    def swapped(item):
        return jnp.logical_and(on_edge, item == last)

    def group_of(item):
        return jnp.where(swapped(item), last - tm, tm)

    def places(item):
        shift = jnp.where(on_last, 1, 0)
        return jnp.where(swapped(item), 0, item + shift), item + 1 + shift

    def skipping(position, mine):
        return position + jnp.where(position >= mine, 1, 0)

    own_boxes = pl.ds(space * box_dev, box_dev)
    barrier = pltpu.get_barrier_semaphore()

    def greet(to_tm):
        for to_space in range(n_space):
            to = (to_tm, to_space)
            pl.semaphore_signal(barrier, inc=1, device_id=to, device_id_type=MESH)

    @pl.when(tm < last)
    def _():
        greet(0)

    for to_tm in range(1, n_tm):
        greet(to_tm)

    fetches = [
        pltpu.make_async_copy(trans_ref, trans_rows, local_sem.at[0]),
        pltpu.make_async_copy(kernel_ref, near_rows, local_sem.at[1]),
        pltpu.make_async_copy(source_ref, sources, local_sem.at[2]),
        pltpu.make_async_copy(near_ref, nears, local_sem.at[3]),
        pltpu.make_async_copy(forward_ref, forward, local_sem.at[4]),
        pltpu.make_async_copy(inverse_ref, inverse, local_sem.at[5]),
    ]
    stagings = [
        pltpu.make_async_copy(signal_ref.at[nth], staged.at[:, nth], stage_sem.at[nth])
        for nth in range(box_dev)
    ]
    for fetch in stagings + fetches:
        fetch.start()
    for staging in stagings:
        staging.wait()

    def place_of(place):
        return landed.at[place, own_boxes]

    def send_in(to_tm, to_space, group, place):
        pltpu.make_async_remote_copy(
            src_ref=staged.at[to_space * n_tm + group],
            dst_ref=place_of(place),
            send_sem=in_send,
            recv_sem=in_recv.at[place],
            device_id=(to_tm, to_space),
            device_id_type=MESH,
        ).start()

    def keep_in(group, place):
        source = staged.at[space * n_tm + group]
        pltpu.make_async_copy(source, place_of(place), in_recv.at[place]).start()

    @pl.when(on_first)
    def _():
        pl.semaphore_wait(barrier, last * n_space)
        for position in reversed(range(last * n_space - 1)):
            far = last * n_space - 2 - position
            peer = skipping(jnp.where(space < n_space // 2, position, far), space * last)
            to_tm, to_space = peer % last, peer // last
            send_in(to_tm, to_space, to_tm, 1)
        for position in reversed(range(n_space - 1)):
            send_in(0, skipping(position, space), last, n_tm)
        keep_in(0, 1)
        keep_in(last, n_tm)
        pl.semaphore_wait(ready, n_space)
        for to_space in reversed(range(n_space)):
            send_in(last, to_space, last, 1)

    @pl.when(on_middle)
    def _():
        pl.semaphore_wait(barrier, peers)
        for position in reversed(range(peers - 1)):
            place = jnp.where(space < n_space // 2, position, peers - 2 - position)
            peer = skipping(place, space * n_tm + tm)
            to_tm, to_space = peer % n_tm, peer // n_tm
            send_in(to_tm, to_space, to_tm, tm + 1)
        keep_in(tm, tm + 1)

        @pl.when(tm == last - 1)
        def _():
            for to_space in reversed(range(n_space)):
                send_in(last, to_space, 0, 0)

    @pl.when(on_last)
    def _():
        pl.semaphore_wait(barrier, peers)
        for to_space in range(n_space):
            pl.semaphore_signal(ready, inc=1, device_id=(0, to_space), device_id_type=MESH)
        for position in reversed(range(last * n_space - 1)):
            far = last * n_space - 2 - position
            peer = skipping(jnp.where(space < n_space // 2, position, far), space * last + last - 1)
            to_tm, to_space = peer % last + 1, peer // last
            send_in(to_tm, to_space, to_tm, n_tm)
        for position in reversed(range(n_space - 1)):
            send_in(last, skipping(position, space), 0, n_tm + 1)
        keep_in(last, n_tm)
        keep_in(0, n_tm + 1)

    for fetch in fetches:
        fetch.wait()

    def respond(lags):
        return jnp.dot(
            lags.astype(jnp.bfloat16), forward[0:LANES, :], preferred_element_type=jnp.float32
        )

    def keep_response(where, both):
        real, imag = both[:, :LANES], both[:, LANES:]
        where[0] = real
        where[1] = imag - real
        where[2] = imag + real

    for turn in range(n_tm):
        first_ray = pl.multiple_of(group_of(item_at(turn)) * SUBLANES, SUBLANES)
        far = respond(
            trans_rows[:, pl.ds(first_ray, SUBLANES), :].reshape(offsets * SUBLANES, LANES)
        )
        for entry in range(offsets):
            these = slice(entry * SUBLANES, (entry + 1) * SUBLANES)
            keep_response(responses.at[turn, entry], far[these])
    near = respond(near_rows[...])
    for slot in range(slots):
        both = jnp.broadcast_to(near[slot : slot + 1, :], (SUBLANES, 2 * LANES))
        keep_response(near_responses.at[slot], both)

    def arrive(place):
        arrived = landed.at[place]
        pltpu.make_async_copy(arrived, arrived, in_recv.at[place]).wait()

    def unpacked(place):
        flat = landed[place].astype(jnp.float32).reshape(boxes * SUBLANES, LANES)
        return flat.astype(jnp.bfloat16)

    def transform(turn):
        earlier, current = places(item_at(turn))
        pair = jnp.concatenate([unpacked(earlier), unpacked(current)], axis=1)
        both = jnp.dot(pair, forward[...], preferred_element_type=jnp.float32)
        spectra[:, 2 * turn] = both[:, :LANES].reshape(boxes, SUBLANES, LANES)
        spectra[:, 2 * turn + 1] = both[:, LANES:].reshape(boxes, SUBLANES, LANES)

    def finish(turn, first):
        targets = [first * box_dev + nth for nth in range(SHARE * box_dev)]
        sums = [None] * len(targets)
        for entry in range(offsets + slots):
            if entry < offsets:
                factors = [responses[turn, entry, part] for part in range(3)]
            else:
                factors = [near_responses[entry - offsets, part] for part in range(3)]
            for place, box in enumerate(targets):
                origin = sources[box, entry] if entry < offsets else nears[entry - offsets, box]
                a, b = (spectra[origin, 2 * turn + part] for part in range(2))
                terms = [factors[0] * (a + b), factors[1] * a, factors[2] * b]
                if entry:
                    terms = [x + y for x, y in zip(sums[place], terms)]
                sums[place] = terms
        real = jnp.concatenate([x - z for x, y, z in sums], axis=0)
        imag = jnp.concatenate([x + y for x, y, z in sums], axis=0)
        spectrum = jnp.concatenate([real, imag], axis=1).astype(jnp.bfloat16)
        field = jnp.dot(spectrum, inverse[...], preferred_element_type=jnp.float32)
        for nth, box in enumerate(targets):
            leaving[turn, box] = field[nth * SUBLANES : (nth + 1) * SUBLANES].astype(jnp.bfloat16)

    def deliver(turn, first):
        item = item_at(turn)
        to_tm = jnp.where(swapped(item), tm, item + jnp.where(on_last, 1, 0))
        target = out_ref.at[:, space * n_tm + group_of(item)]
        own_line = to_tm == tm
        own_here = jnp.logical_and(own_line, space // SHARE == first // SHARE)

        def source(to_space):
            return leaving.at[turn, pl.ds(to_space * box_dev, box_dev)]

        def send_out(to_space):
            pltpu.make_async_remote_copy(
                src_ref=source(to_space),
                dst_ref=target,
                send_sem=out_send,
                recv_sem=out_recv,
                device_id=(to_tm, to_space),
                device_id_type=MESH,
            ).start()

        @pl.when(jnp.logical_not(own_here))
        def _():
            for nth in range(SHARE):
                send_out(first + nth)

        @pl.when(own_here)
        def _():
            for position in range(SHARE - 1):
                send_out(first + skipping(position, space - first))
            pltpu.make_async_copy(source(space), target, out_recv).start()

    @pl.when(tm < last)
    def _():
        landed[0] = jnp.zeros(landed.shape[1:], jnp.bfloat16)

    for turn in range(n_tm):
        for line in range(n_tm):
            if awaited(line, turn):

                @pl.when(tm == line)
                def _():
                    for place in awaited(line, turn):
                        arrive(place)

        transform(turn)

        for first in range(0, n_space, SHARE):
            finish(turn, first)
            deliver(turn, first)

    def settle(pieces, sem):
        sent = staged.at[pl.ds(0, pieces)]
        pltpu.make_async_copy(sent, sent, sem).wait()

    @pl.when(on_first)
    def _():
        settle(last * n_space - 1 + n_space - 1, in_send)
        settle(n_space, in_send)

    @pl.when(on_middle)
    def _():
        settle(peers - 1, in_send)

        @pl.when(tm == last - 1)
        def _():
            settle(n_space, in_send)

    @pl.when(on_last)
    def _():
        settle(last * n_space - 1 + n_space - 1, in_send)

    pltpu.make_async_copy(out_ref, out_ref, out_recv).wait()

    @pl.when(on_middle)
    def _():
        settle(peers - 1, out_send)

    @pl.when(on_edge)
    def _():
        settle(peers - 2, out_send)


def fused_body(signal, source_boxes, near_boxes, trans_kernel, near_kernel):
    n_tm, n_space = lax.axis_size("tm"), lax.axis_size("space")
    peers = n_tm * n_space
    box_dev, rays, samples = signal.shape
    boxes = box_dev * n_space
    offsets, slots = trans_kernel.shape[0], near_kernel.shape[0]
    rows = n_tm * boxes
    grouped = signal.reshape(box_dev, peers, SUBLANES, samples)
    forward, inverse = spectral_tables(samples)
    operands = (
        grouped, source_boxes, near_boxes.T, trans_kernel, near_kernel, forward, inverse
    )
    hbm = pl.BlockSpec(memory_space=pltpu.HBM)
    field = pl.pallas_call(
        functools.partial(fused_kernel, n_tm, n_space),
        out_shape=pltpu.VMEM(grouped.shape, jnp.bfloat16),
        in_specs=[hbm] * len(operands),
        out_specs=pl.BlockSpec(memory_space=pl.ANY),
        scratch_shapes=[
            pltpu.VMEM((peers, box_dev, SUBLANES, LANES), jnp.bfloat16),
            pltpu.VMEM((n_tm + 2, boxes, SUBLANES, LANES), jnp.bfloat16),
            pltpu.VMEM((boxes, 2 * n_tm, SUBLANES, LANES), jnp.float32),
            pltpu.VMEM((n_tm, offsets, 3, SUBLANES, LANES), jnp.float32),
            pltpu.VMEM((slots, 3, SUBLANES, LANES), jnp.float32),
            pltpu.VMEM(trans_kernel.shape, jnp.float32),
            pltpu.VMEM((slots, LANES), jnp.float32),
            pltpu.VMEM(forward.shape, jnp.bfloat16),
            pltpu.VMEM(inverse.shape, jnp.bfloat16),
            pltpu.VMEM((n_tm, boxes, SUBLANES, LANES), jnp.bfloat16),
            pltpu.SMEM(source_boxes.shape, jnp.int32),
            pltpu.SMEM(near_boxes.shape[::-1], jnp.int32),
            pltpu.SemaphoreType.DMA,
            pltpu.SemaphoreType.DMA((n_tm + 2,)),
            pltpu.SemaphoreType.DMA,
            pltpu.SemaphoreType.DMA,
            pltpu.SemaphoreType.DMA((6,)),
            pltpu.SemaphoreType.DMA((box_dev,)),
            pltpu.SemaphoreType.REGULAR,
        ],
        compiler_params=pltpu.CompilerParams(
            collective_id=0, has_side_effects=True, vmem_limit_bytes=60*1024*1024
        ),
    )(*[pltpu.with_memory_space_constraint(x, pltpu.HBM) for x in operands])
    return field.reshape(signal.shape)


def routed(signal, source_boxes, near_boxes, trans_kernel, near_kernel):
    n_tm, n_space = lax.axis_size("tm"), lax.axis_size("space")
    box_dev, rays, samples = signal.shape
    rows = n_tm * n_space * box_dev
    fits = n_tm == 4 and n_space % SHARE == 0 and rays == n_tm * n_space * SUBLANES and samples == LANES and rows <= 2 * LANES
    chosen = fused_body if fits else body
    return chosen(signal, source_boxes, near_boxes, trans_kernel, near_kernel)


def solution(mesh):
    in_specs = (P("space", None, "tm"), P(), P(), P(None, "space", None), P())
    out_specs = P("space", None, "tm")
    return jax.shard_map(
        routed, mesh=mesh, in_specs=in_specs, out_specs=out_specs, check_vma=False
    )
```
